512 devices in a mesh: tiles: 256 (over y, z, x), rep: 2 (over core).
Axes of the slice: x: 4, y: 4, z: 16, core: 2. Of those that a mesh axis runs over, the one named last changes fastest.
Arguments:
- members: bfloat16 [8192, 80, 256], P(('tiles', 'rep')), may hold values from -1350 to 1350
- initial: bfloat16 [8192, 32, 256], P(('tiles', 'rep')), may hold values from -6 to 6
- wet_counts: int32 [8192], P(('tiles', 'rep')), may hold values from 1 to 256, as said below
- tile_coords: int32 [8192, 2], P(('tiles', 'rep')), may hold values from 0 to 1023, as said below
- neighbours: int32 [8192, 9], P(('tiles', 'rep')), may hold values from -1 to 8191, as said below
Outputs:
- leading: float32 [8192, 32, 256], P(('tiles', 'rep'))
The draws below stay inside these ranges and needn't reach their ends.
Inputs may be any that keep to these rules, and one draw needn't show every extreme that they name: `wet_counts`: each tile's count of wet points; some tiles are all wet. `tile_coords`: tiles form a strip of columns of 8 consecutive tiles; the first entry is the column, consecutive columns are offset by at most one tile in the second entry. `neighbours`: each tile lists, in increasing order and followed by -1 padding, every tile whose two entries of tile_coords differ from its own by at most one, itself included; the list is symmetric.
All inputs are finite; a program needn't handle non-finite values.
Results may differ from the reference program's by a relative error of at most 0.00065.
The reference program's roundings to bfloat16 on the way count: a program that leaves them out, or rounds other values in their place, can miss the bound.
Values may be sent and summed in bfloat16 or wider, within the bound.
No kernel may reach another device: no remote copies, remote signals or barrier semaphores. Data moves between devices by JAX's collectives and lax.ppermute only.
A program may use at most 128 MiB of HBM per device.

```python
import math
import jax
import jax.numpy as jnp
from jax import lax

TILE_SIDE = 16
GRID_POINTS = 256
MEMBERS = 80
RANK = 32
NBR = 9
COLW = 8
ITERS = 2
TILE_TOTAL = 8192


def tile_layout(key):
    column_count = TILE_TOTAL // COLW
    layout_key = jax.random.fold_in(key, 101)
    column_ids = jnp.arange(column_count, dtype=jnp.int32)
    drawn_shift = jax.random.randint(layout_key, (column_count,), 0, 2, dtype=jnp.int32)
    shifts = jnp.where(column_ids == 0, 1, jnp.where(column_ids == 1, 0, drawn_shift)).astype(jnp.int32)
    tile_ids = jnp.arange(TILE_TOTAL, dtype=jnp.int32)
    across = tile_ids // COLW
    upward = tile_ids % COLW + shifts[across]
    places = jnp.stack([across, upward], axis=1)
    offsets = jnp.arange(-(COLW + 2), COLW + 3, dtype=jnp.int32)
    candidate = tile_ids[:, None] + offsets[None, :]
    inside = (candidate >= 0) & (candidate < TILE_TOTAL)
    clipped = jnp.clip(candidate, 0, TILE_TOTAL - 1)
    adjacent = inside & (jnp.abs(across[clipped] - across[:, None]) <= 1) & (jnp.abs(upward[clipped] - upward[:, None]) <= 1)
    position = jnp.cumsum(adjacent.astype(jnp.int32), axis=1) - 1
    position = jnp.where(adjacent, position, NBR)
    neighbour_lists = jnp.full((TILE_TOTAL, NBR), -1, dtype=jnp.int32)
    neighbour_lists = neighbour_lists.at[tile_ids[:, None], position].set(candidate, mode='drop')
    return (places, neighbour_lists)


def draw_tile_coords(key, part):
    return tile_layout(key)[0]


def draw_neighbours(key, part):
    return tile_layout(key)[1]


def draw_wet_counts(key, part):
    point_counts = jax.random.randint(jax.random.fold_in(key, 5), (TILE_TOTAL,), 1, GRID_POINTS + 1, dtype=jnp.int32)
    open_ocean = jax.random.randint(jax.random.fold_in(key, 6), (TILE_TOTAL,), 0, 3, dtype=jnp.int32) == 0
    tile_ids = jnp.arange(TILE_TOTAL, dtype=jnp.int32)
    return jnp.where(open_ocean | (tile_ids % 5 == 0), GRID_POINTS, point_counts).astype(jnp.int32)


def draw_members(key, part):
    perturb = jnp.clip(jax.random.normal(jax.random.fold_in(key, 1), (TILE_TOTAL, MEMBERS, GRID_POINTS), jnp.float32), -4.0, 4.0)
    tile_scale = jnp.exp(jax.random.uniform(jax.random.fold_in(key, 2), (TILE_TOTAL, 1, 1), jnp.float32, 0.0, math.log(10.0)))
    tile_ids = jnp.arange(TILE_TOTAL, dtype=jnp.int32)
    growth = (1.0 + 2.0 * tile_ids.astype(jnp.float32) / max(TILE_TOTAL - 1, 1)).reshape(TILE_TOTAL, 1, 1)
    rim_tiles = (tile_ids < 3 * COLW) | (tile_ids >= TILE_TOTAL - 3 * COLW)
    edge_boost = jnp.where(rim_tiles, 3.0, 1.0).astype(jnp.float32).reshape(TILE_TOTAL, 1, 1)
    return (perturb * tile_scale * growth * edge_boost).astype(jnp.bfloat16)


def levels(stream_key, extent, pieces, smallest, high):
    def one(axis_at, shards_of):
        heights = jax.random.uniform(jax.random.fold_in(jax.random.fold_in(stream_key, 6), axis_at), (shards_of,), jnp.float32, smallest / len(pieces), high / len(pieces))
        return jnp.repeat(jnp.exp(heights), extent[axis_at] // shards_of).reshape((-1,) + (1,) * (len(extent) - axis_at - 1))

    loudness = one(*pieces[0])
    for cut in pieces[1:]:
        loudness = loudness * one(*cut)
    return loudness


def bell_draw(stream_key, dims, deviation, reach, shards=(), kind=jnp.bfloat16):
    array = deviation * jax.random.normal(stream_key, dims, jnp.float32)
    if shards:
        array = array * levels(stream_key, dims, shards, -0.22, 0.18)
    return jnp.clip(array, -reach, reach).astype(kind)


def setup_inputs(seed: int = 0) -> dict:
    seeds = jax.random.split(jax.random.key(seed), 6)
    members = draw_members(jax.random.fold_in(seeds[5], 71), 0)
    initial = bell_draw(seeds[1], (TILE_TOTAL, RANK, GRID_POINTS), 1.0, 6.0, ((0, 512),))
    wet_counts = draw_wet_counts(jax.random.fold_in(seeds[5], 71), 0)
    tile_coords = draw_tile_coords(jax.random.fold_in(seeds[5], 71), 0)
    neighbours = draw_neighbours(jax.random.fold_in(seeds[5], 71), 0)
    return {"members": members, "initial": initial, "wet_counts": wet_counts, "tile_coords": tile_coords, "neighbours": neighbours}


def gaspari(distance):
    scaled = distance / (0.5 * TILE_SIDE)
    clamped = jnp.maximum(scaled, 1.0)
    inner_part = (((-0.25 * scaled + 0.5) * scaled + 0.625) * scaled - 5.0 / 3.0) * scaled * scaled + 1.0
    outer_part = ((((scaled / 12.0 - 0.5) * scaled + 0.625) * scaled + 5.0 / 3.0) * scaled - 5.0) * scaled + 4.0 - 2.0 / (3.0 * clamped)
    return jnp.where(scaled <= 1.0, inner_part, jnp.where(scaled <= 2.0, outer_part, 0.0))

def distances(place_one, place_two):
    points = jnp.arange(TILE_SIDE * TILE_SIDE, dtype=jnp.int32)
    across = points // TILE_SIDE
    along_row = points % TILE_SIDE
    row_one = place_one[..., 0:1] * TILE_SIDE + across
    col_one = place_one[..., 1:2] * TILE_SIDE + along_row
    row_two = place_two[..., 0:1] * TILE_SIDE + across
    col_two = place_two[..., 1:2] * TILE_SIDE + along_row
    delta_row = (row_one[..., :, None] - row_two[..., None, :]).astype(jnp.float32)
    delta_col = (col_one[..., :, None] - col_two[..., None, :]).astype(jnp.float32)
    return jnp.sqrt(delta_row * delta_row + delta_col * delta_col)

def covariance_apply(masked, tile_coords, neighbours, current):

    def one_tile(inputs):
        rows_one, place_one, listed = inputs
        usable = listed >= 0
        safe_index = jnp.maximum(listed, 0).astype(jnp.int32)
        product = jnp.einsum('mi,smj->sij', rows_one.astype(jnp.float32), masked[safe_index].astype(jnp.float32))
        weight = gaspari(distances(place_one[None, :], tile_coords[safe_index]))
        blocks = (product * weight / (MEMBERS - 1.0)).astype(jnp.bfloat16)
        contrib = jnp.einsum('skj,sij->ski', current[safe_index].astype(jnp.float32), blocks.astype(jnp.float32))
        return lax.optimization_barrier(jnp.sum(jnp.where(usable[:, None, None], contrib, 0.0), axis=0))
    return lax.map(one_tile, (masked, tile_coords, neighbours))

def orthonormal(applied_product):
    summed_gram = jnp.einsum('brg,bsg->rs', applied_product, applied_product, precision=lax.Precision.HIGHEST) / (TILE_TOTAL * GRID_POINTS * 1.0)
    factor = jnp.linalg.cholesky(summed_gram)
    inverse_factor = jax.scipy.linalg.solve_triangular(factor, jnp.eye(summed_gram.shape[0], dtype=jnp.float32), lower=True)
    return jnp.einsum('fy,ryc->rfc', inverse_factor, applied_product, precision=lax.Precision.HIGHEST)

def reference(members, initial, wet_counts, tile_coords, neighbours):
    wet_mask = jnp.arange(GRID_POINTS, dtype=jnp.int32)[None, :] < wet_counts[:, None]
    masked = jnp.where(wet_mask[:, None, :], members, jnp.zeros_like(members))
    current = initial
    fresh = jnp.zeros(initial.shape, jnp.float32)
    for sweep_index in range(ITERS):
        applied_product = covariance_apply(masked, tile_coords, neighbours, current)
        fresh = orthonormal(applied_product)
        current = fresh.astype(jnp.bfloat16)
    return fresh
```

```python
import functools

import jax
import jax.numpy as jnp
from jax import lax
from jax.experimental import pallas as pl
from jax.experimental.pallas import tpu as pltpu
from jax.sharding import Mesh
from jax.sharding import PartitionSpec as P

SIDE = 16
COLW = 8
SPLIT = (4, 16, 4)
TILES_REP = ("tiles_0", "tiles_1", "tiles_2", "rep")
PLANE = ("tiles_0", "tiles_2", "rep")
LINE = ("tiles_1",)
PAD = 2
SLOTS = COLW + 2 * PAD
DEPTH = 128
ROWS = 64
F32 = jnp.float32
BF16 = jnp.bfloat16
VMEM_LIMIT = 56 * 1024 * 1024


def gaspari(scaled):
    clamped = jnp.maximum(scaled, 1.0)
    inner = (((-0.25 * scaled + 0.5) * scaled + 0.625) * scaled - 5.0 / 3.0) * scaled * scaled + 1.0
    outer = (
        ((((scaled / 12.0 - 0.5) * scaled + 0.625) * scaled + 5.0 / 3.0) * scaled - 5.0) * scaled
        + 4.0
        - 2.0 / (3.0 * clamped)
    )
    return jnp.where(scaled <= 1.0, inner, jnp.where(scaled <= 2.0, outer, 0.0))


def make_tapers(table_ref, wide_ref, members):
    shape = (SIDE, 64 * SIDE)
    lane = lax.broadcasted_iota(jnp.int32, shape, 1)
    sub = lax.broadcasted_iota(jnp.int32, shape, 0)
    apart_row = (2 * SIDE - 1 - lane // SIDE).astype(F32)
    for k in range(3):
        apart_col = (SIDE * (k - 1) + sub - lane % SIDE).astype(F32)
        distance = jnp.sqrt(apart_row * apart_row + apart_col * apart_col)
        wide_ref[k] = gaspari(distance / (0.5 * SIDE)) / (members - 1.0)
    for d in range(3):
        for k in range(3):
            for row in range(SIDE):
                start = SIDE * (2 * SIDE - 1 - SIDE * (d - 1) - row)
                table_ref[d * 3 + k, row * SIDE : (row + 1) * SIDE, :] = wide_ref[
                    k, :, start : start + SIDE * SIDE
                ]


def split3(x):
    high = x.astype(BF16)
    rest = x - high.astype(F32)
    mid = rest.astype(BF16)
    low = (rest - mid.astype(F32)).astype(BF16)
    return high, mid, low


def block_and_apply(turned_ref, at, right, table, block_ref, rows_here):
    for start in range(0, SIDE * SIDE, ROWS):
        product = jnp.dot(turned_ref[at, start : start + ROWS, :], right, preferred_element_type=F32)
        block_ref[start : start + ROWS, :] = (product * table[start : start + ROWS, :]).astype(BF16)
    return jnp.dot(rows_here, block_ref[...], preferred_element_type=F32)


def gram_add(gram_ref, applied):
    parts = jnp.concatenate(split3(applied), 0)
    gram_ref[...] += lax.dot_general(parts, parts, (((1,), (1,)), ((), ())), preferred_element_type=F32)


def gram_packed(gram_ref, rank):
    full = gram_ref[...]

    def piece(a, b):
        return full[a * rank : (a + 1) * rank, b * rank : (b + 1) * rank]

    small = piece(0, 2) + piece(2, 0) + piece(1, 1) + (piece(1, 2) + piece(2, 1))
    total = piece(0, 0) + (piece(0, 1) + piece(1, 0) + small)
    return jnp.concatenate([total[8 * q : 8 * q + 8, :] for q in range(rank // 8)], 1)


def inverse_factor(packed, rank, total_points):
    gram = jnp.concatenate([packed[:, rank * q : rank * (q + 1)] for q in range(rank // 8)], 0)
    gram = gram / total_points
    work = jnp.concatenate([gram, jnp.zeros((rank, 128 - rank), F32)], 1)
    lane = lax.broadcasted_iota(jnp.int32, (rank, 128), 1)
    sub = lax.broadcasted_iota(jnp.int32, (rank, 128), 0)
    work = jnp.where(lane == sub + rank, 1.0, work)
    for step in range(rank - 1):
        top = (step + 1) // 8 * 8
        row = work[step : step + 1, :]
        pivot = work[step : step + 1, step : step + 1]
        below = work[top:, :]
        factor = below[:, step : step + 1] / pivot
        below = jnp.where(sub[top:, :] > step, below - factor * row, below)
        work = jnp.concatenate([work[:top, :], below], 0) if top else below
    diagonal = jnp.sum(jnp.where(lane == sub, work, 0.0), axis=1, keepdims=True)
    return work[:, rank : 2 * rank] / jnp.sqrt(diagonal)


def fresh_left(inverse):
    h1, h2, h3 = split3(inverse)
    return jnp.concatenate([h1, h1, h2, h1, h2, h3, h2, h3], 1)


def fresh_of(left, applied):
    a1, a2, a3 = split3(applied)
    right = jnp.concatenate([a1, a2, a1, a3, a2, a1, a3, a2], 0)
    return jnp.dot(left, right, preferred_element_type=F32)


def clear_pads(ref, columns):
    for column in range(columns):
        for slot in list(range(PAD)) + list(range(SLOTS - PAD, SLOTS)):
            ref[column * SLOTS + slot] = jnp.zeros(ref.shape[1:], ref.dtype)


def turn_in(turned_ref, at, rows):
    depth = rows.shape[0]
    padded = jnp.concatenate([rows, jnp.zeros((DEPTH - depth, rows.shape[1]), F32)], 0)
    turned_ref[at] = jnp.transpose(padded).astype(BF16)
    return padded.astype(BF16)


def own_kernel(
    wet_ref, coord_ref, members_ref, initial_ref,
    table_ref, padded_ref, block_ref, part_ref,
    wide_ref, turned_ref, iter_ref,
):
    step = pl.program_id(0)
    count = members_ref.shape[1]

    @pl.when(step == 0)
    def _():
        make_tapers(table_ref, wide_ref, float(count))
        clear_pads(turned_ref, 2)
        clear_pads(iter_ref, 2)

        @pl.loop(0, 2 * COLW)
        def _(tile):
            at = tile + PAD + jnp.where(tile >= COLW, 2 * PAD, 0)
            lane = lax.broadcasted_iota(jnp.int32, members_ref.shape[1:], 1)
            rows = jnp.where(lane < wet_ref[tile], members_ref[tile].astype(F32), 0.0)
            padded_ref[tile] = turn_in(turned_ref, at, rows)
            iter_ref[at] = initial_ref[tile]

    shift = jnp.clip(coord_ref[0, 1] - coord_ref[COLW, 1], -1, 1)
    for column in range(2):
        right = padded_ref[column * COLW + step]
        total = None
        for slot in range(6):
            k = slot % 3
            if slot < 3:
                at = column * SLOTS + PAD + step + k - 1
                d = 1
            else:
                moved = shift if column == 0 else -shift
                at = (1 - column) * SLOTS + PAD + step + moved + k - 1
                d = 2 if column == 0 else 0
            here = block_and_apply(
                turned_ref, at, right, table_ref.at[d * 3 + k],
                block_ref.at[0, column * 6 + slot], iter_ref[at],
            )
            total = here if total is None else total + here
        part_ref[0, column] = total


def halo_kernel(
    listed_ref, padded_ref, table_ref, part_ref, left_ref, right_ref,
    block_ref, first_ref, second_ref, gram_out_ref,
    turned_ref, iter_ref, gram_ref,
):
    step = pl.program_id(0)
    rank = iter_ref.shape[1]
    count = left_ref.shape[1] - rank

    @pl.when(step == 0)
    def _():
        clear_pads(turned_ref, 2)
        clear_pads(iter_ref, 2)
        gram_ref[...] = jnp.zeros_like(gram_ref)
        for column, ref in enumerate((left_ref, right_ref)):

            @pl.loop(0, COLW)
            def _(tile):
                at = column * SLOTS + PAD + tile
                turn_in(turned_ref, at, ref[tile, :count, :].astype(F32))
                iter_ref[at] = ref[tile, count:, :]

    middle = COLW // 2 - 1
    before = listed_ref[middle, 0] - listed_ref[middle, 3] + COLW
    after = listed_ref[COLW + middle, 8] - listed_ref[COLW + middle, 5] - COLW
    for column, moved in enumerate((before, after)):
        moved = jnp.clip(moved, -1, 1)
        right = padded_ref[column * COLW + step]
        total = part_ref[0, column]
        for k in range(3):
            at = column * SLOTS + PAD + step + moved + k - 1
            d = 0 if column == 0 else 2
            total = total + block_and_apply(
                turned_ref, at, right, table_ref.at[d * 3 + k],
                block_ref.at[0, column * 3 + k], iter_ref[at],
            )
        (first_ref, second_ref)[column][0] = total
        gram_add(gram_ref, total)

    @pl.when(step == COLW - 1)
    def _():
        gram_out_ref[...] = jnp.broadcast_to(gram_packed(gram_ref, rank)[None], gram_out_ref.shape)


def again_kernel(
    total_points,
    coord_ref, listed_ref, grams_ref, first_ref, second_ref, left_ref, right_ref, own_hbm, halo_hbm,
    out_ref, gram_out_ref,
    own_ref, halo_ref, iter_ref, gram_ref, sem,
):
    rank = first_ref.shape[1]

    def copies(r):
        return (
            pltpu.make_async_copy(own_hbm.at[r], own_ref.at[r], sem.at[0, r]),
            pltpu.make_async_copy(halo_hbm.at[r], halo_ref.at[r], sem.at[1, r]),
        )

    for r in range(COLW):
        for copy in copies(r):
            copy.start()
    clear_pads(iter_ref, 4)
    gram_ref[...] = jnp.zeros_like(gram_ref)
    left = fresh_left(inverse_factor(jnp.sum(grams_ref[...], 0), rank, total_points))

    @pl.loop(0, COLW)
    def _(r):
        for column, ref in enumerate((left_ref, first_ref, second_ref, right_ref)):
            iter_ref[column * SLOTS + PAD + r] = fresh_of(left, ref[r]).astype(BF16)

    shift = jnp.clip(coord_ref[0, 1] - coord_ref[COLW, 1], -1, 1)
    middle = COLW // 2 - 1
    before = jnp.clip(listed_ref[middle, 0] - listed_ref[middle, 3] + COLW, -1, 1)
    after = jnp.clip(listed_ref[COLW + middle, 8] - listed_ref[COLW + middle, 5] - COLW, -1, 1)

    @pl.loop(0, COLW)
    def _(r):
        for copy in copies(r):
            copy.wait()
        for column in range(2):
            home = (column + 1) * SLOTS + PAD + r
            own_move = SLOTS + shift if column == 0 else -SLOTS - shift
            halo_move = -SLOTS + before if column == 0 else SLOTS + after
            total = None
            for slot in range(9):
                k = slot % 3 - 1
                if slot < 6:
                    at = home + k + (own_move if slot >= 3 else 0)
                    block = own_ref[r, column * 6 + slot]
                else:
                    at = home + k + halo_move
                    block = halo_ref[r, column * 3 + slot - 6]
                here = jnp.dot(iter_ref[at], block, preferred_element_type=F32)
                total = here if total is None else total + here
            out_ref[column * COLW + r] = total
            gram_add(gram_ref, total)

    gram_out_ref[...] = jnp.broadcast_to(gram_packed(gram_ref, rank)[None], gram_out_ref.shape)


def last_kernel(total_points, grams_ref, applied_ref, out_ref):
    rank = applied_ref.shape[1]
    left = fresh_left(inverse_factor(jnp.sum(grams_ref[...], 0), rank, total_points))

    @pl.loop(0, applied_ref.shape[0])
    def _(tile):
        out_ref[tile] = fresh_of(left, applied_ref[tile])


def fold_kernel(in_ref, out_ref):
    out_ref[...] = jnp.broadcast_to(jnp.sum(in_ref[...], 0)[None], out_ref.shape)


def cost(flops, moved):
    return pl.CostEstimate(flops=flops, bytes_accessed=moved, transcendentals=0)


def whole(shape):
    return pl.BlockSpec(shape, lambda r: (0,) * len(shape))


def per_step(shape):
    return pl.BlockSpec((1, *shape[1:]), lambda r: (r,) + (0,) * (len(shape) - 1))


SMEM = pl.BlockSpec(memory_space=pltpu.SMEM)
VMEM = pl.BlockSpec(memory_space=pltpu.VMEM)
PARAMS = pltpu.CompilerParams(vmem_limit_bytes=VMEM_LIMIT)


def shifted(shard, by):
    length = lax.axis_size(TILES_REP)
    pairs = [(i, i + by) for i in range(length) if 0 <= i + by < length]
    return lax.ppermute(shard, TILES_REP, pairs)


def exchanged(shard, axes):
    return lax.all_to_all(shard, axes, split_axis=0, concat_axis=0, tiled=True)


def gathered(copies):
    line = lax.axis_size(LINE)
    plane = exchanged(copies, PLANE)
    summed = pl.pallas_call(
        fold_kernel,
        out_shape=jax.ShapeDtypeStruct((line, *copies.shape[1:]), F32),
        in_specs=[VMEM],
        out_specs=VMEM,
    )(plane)
    return exchanged(summed, LINE)


def local(members, initial, wet_counts, tile_coords, neighbours):
    tiles, count, points = members.shape
    rank = initial.shape[1]
    assert tiles == 2 * COLW and points == SIDE * SIDE and rank == 32
    shape = jax.ShapeDtypeStruct
    total_points = float(tiles * lax.axis_size(TILES_REP) * points)
    plane = lax.axis_size(PLANE)
    packed = (8, rank * rank // 8)

    lane = jnp.arange(points, dtype=jnp.int32)
    masked = jnp.where((lane[None, :] < wet_counts[:, None])[:, None, :], members, jnp.zeros_like(members))
    from_right = shifted(jnp.concatenate([masked[:COLW], initial[:COLW]], 1), -1)
    from_left = shifted(jnp.concatenate([masked[COLW:], initial[COLW:]], 1), 1)

    table_s, padded_s = shape((9, points, points), F32), shape((tiles, DEPTH, points), BF16)
    own_s, part_s = shape((COLW, 12, points, points), BF16), shape((COLW, 2, rank, points), F32)
    halo_s, half_s = shape((COLW, 6, points, points), BF16), shape((COLW, rank, points), F32)
    table, padded, own_blocks, part = pl.pallas_call(
        own_kernel,
        grid=(COLW,),
        out_shape=(table_s, padded_s, own_s, part_s),
        in_specs=[SMEM, SMEM, whole(members.shape), whole(initial.shape)],
        out_specs=(whole(table_s.shape), whole(padded_s.shape), per_step(own_s.shape), per_step(part_s.shape)),
        scratch_shapes=[
            pltpu.VMEM((3, SIDE, 64 * SIDE), F32),
            pltpu.VMEM((2 * SLOTS, points, DEPTH), BF16),
            pltpu.VMEM((2 * SLOTS, rank, points), BF16),
        ],
        compiler_params=PARAMS,
        cost_estimate=cost(96 * 2 * points * points * (DEPTH + rank), 40_000_000),
        name="own_blocks",
    )(wet_counts, tile_coords, members, initial)

    halo_blocks, first, second, copies = pl.pallas_call(
        halo_kernel,
        grid=(COLW,),
        out_shape=(halo_s, half_s, half_s, shape((plane, *packed), F32)),
        in_specs=[
            SMEM, whole(padded_s.shape), whole(table_s.shape), per_step(part_s.shape),
            whole(from_left.shape), whole(from_right.shape),
        ],
        out_specs=(
            per_step(halo_s.shape), per_step(half_s.shape), per_step(half_s.shape),
            whole((plane, *packed)),
        ),
        scratch_shapes=[
            pltpu.VMEM((2 * SLOTS, points, DEPTH), BF16),
            pltpu.VMEM((2 * SLOTS, rank, points), BF16),
            pltpu.VMEM((3 * rank, 3 * rank), F32),
        ],
        compiler_params=PARAMS,
        cost_estimate=cost(48 * 2 * points * points * (DEPTH + rank), 20_000_000),
        name="halo_blocks",
    )(neighbours, padded, table, part, from_left, from_right)

    after = shifted(first, -1)
    before = shifted(second, 1)
    applied, copies = pl.pallas_call(
        functools.partial(again_kernel, total_points),
        out_shape=(shape((tiles, rank, points), F32), shape((plane, *packed), F32)),
        in_specs=[SMEM, SMEM, VMEM, VMEM, VMEM, VMEM, VMEM]
        + [pl.BlockSpec(memory_space=pl.ANY)] * 2,
        out_specs=(VMEM, VMEM),
        scratch_shapes=[
            pltpu.VMEM(own_s.shape, BF16),
            pltpu.VMEM(halo_s.shape, BF16),
            pltpu.VMEM((4 * SLOTS, rank, points), BF16),
            pltpu.VMEM((3 * rank, 3 * rank), F32),
            pltpu.SemaphoreType.DMA((2, COLW)),
        ],
        compiler_params=PARAMS,
        name="apply_again",
    )(tile_coords, neighbours, gathered(copies), first, second, before, after, own_blocks, halo_blocks)

    return pl.pallas_call(
        functools.partial(last_kernel, total_points),
        out_shape=shape((tiles, rank, points), F32),
        in_specs=[VMEM, VMEM],
        out_specs=VMEM,
        name="last_fresh",
    )(gathered(copies), applied)


def solution(mesh):
    split = Mesh(mesh.devices.reshape(*SPLIT, mesh.shape["rep"]), TILES_REP)
    return jax.shard_map(
        local,
        mesh=split,
        in_specs=(
            P(TILES_REP, None, None),
            P(TILES_REP, None, None),
            P(TILES_REP),
            P(TILES_REP, None),
            P(TILES_REP, None),
        ),
        out_specs=P(TILES_REP, None, None),
        check_vma=False,
    )
```

```python
import functools

import jax
import jax.numpy as jnp
from jax import lax
from jax.experimental import pallas as pl
from jax.experimental.pallas import tpu as pltpu
from jax.sharding import Mesh
from jax.sharding import PartitionSpec as P

SIDE = 16
COLW = 8
SPLIT = (4, 16, 4)
TILES_REP = ("tiles_0", "tiles_1", "tiles_2", "rep")
PLANE = ("tiles_0", "tiles_2", "rep")
LINE = ("tiles_1",)
PAD = 2
SLOTS = COLW + 2 * PAD
DEPTH = 128
F32 = jnp.float32
BF16 = jnp.bfloat16
VMEM_LIMIT = 20 * 1024 * 1024


def gaspari(scaled):
    clamped = jnp.maximum(scaled, 1.0)
    inner = (((-0.25 * scaled + 0.5) * scaled + 0.625) * scaled - 5.0 / 3.0) * scaled * scaled + 1.0
    outer = (
        ((((scaled / 12.0 - 0.5) * scaled + 0.625) * scaled + 5.0 / 3.0) * scaled - 5.0) * scaled
        + 4.0
        - 2.0 / (3.0 * clamped)
    )
    return jnp.where(scaled <= 1.0, inner, jnp.where(scaled <= 2.0, outer, 0.0))


def make_tapers(table_ref, wide_ref, members):
    shape = (SIDE, 64 * SIDE)
    lane = lax.broadcasted_iota(jnp.int32, shape, 1)
    sub = lax.broadcasted_iota(jnp.int32, shape, 0)
    apart_row = (2 * SIDE - 1 - lane // SIDE).astype(F32)
    for k in range(3):
        apart_col = (SIDE * (k - 1) + sub - lane % SIDE).astype(F32)
        distance = jnp.sqrt(apart_row * apart_row + apart_col * apart_col)
        wide_ref[k] = gaspari(distance / (0.5 * SIDE)) / (members - 1.0)
    per_group = 128 // SIDE
    for k in range(3):
        wide = wide_ref[k]
        for turn in range(per_group):
            rolled = pltpu.roll(wide, 64 * SIDE - turn * SIDE, 1) if turn else wide
            for d in range(3):
                for row in range(SIDE):
                    first = 2 * SIDE - 1 - SIDE * (d - 1) - row
                    if first % per_group == turn:
                        start = (first - turn) * SIDE
                        table_ref[d * 3 + k, row * SIDE : (row + 1) * SIDE, :] = rolled[
                            :, start : start + SIDE * SIDE
                        ]


def split3(x):
    high = x.astype(BF16)
    rest = x - high.astype(F32)
    mid = rest.astype(BF16)
    low = (rest - mid.astype(F32)).astype(BF16)
    return high, mid, low


def make_blocks(turned_ref, at, right, tables, block_ref, first):
    points = right.shape[1]
    count = len(tables)
    for n, table in enumerate(tables):
        product = jnp.dot(turned_ref[at + n], right, preferred_element_type=F32)
        block_ref[first + n] = (product * table[...]).astype(BF16)


def times(rows, block):
    return jnp.dot(rows, block, preferred_element_type=F32)


def times_turned(rows, block):
    return lax.dot_general(rows, block, (((1,), (1,)), ((), ())), preferred_element_type=F32)


def gram_add(gram_ref, applied):
    parts = jnp.concatenate(split3(applied), 0)
    gram_ref[...] += lax.dot_general(parts, parts, (((1,), (1,)), ((), ())), preferred_element_type=F32)


def gram_packed(gram_ref, rank):
    full = gram_ref[...]

    def piece(a, b):
        return full[a * rank : (a + 1) * rank, b * rank : (b + 1) * rank]

    small = piece(0, 2) + piece(2, 0) + piece(1, 1) + (piece(1, 2) + piece(2, 1))
    total = piece(0, 0) + (piece(0, 1) + piece(1, 0) + small)
    return jnp.concatenate([total[8 * q : 8 * q + 8, :] for q in range(rank // 8)], 1)


def inverse_factor(packed, rank, total_points):
    gram = jnp.concatenate([packed[:, rank * q : rank * (q + 1)] for q in range(rank // 8)], 0)
    gram = gram / total_points
    work = jnp.concatenate([gram, jnp.zeros((rank, 128 - rank), F32)], 1)
    lane = lax.broadcasted_iota(jnp.int32, (rank, 128), 1)
    sub = lax.broadcasted_iota(jnp.int32, (rank, 128), 0)
    work = jnp.where(lane == sub + rank, 1.0, work)
    for step in range(0, rank - 2, 2):
        top = (step + 2) // 8 * 8
        row0, row1 = work[step : step + 1, :], work[step + 1 : step + 2, :]
        p00, p01 = row0[:, step : step + 1], row0[:, step + 1 : step + 2]
        p11 = row1[:, step + 1 : step + 2]
        scale = 1.0 / (p00 * p11 - p01 * p01)
        lead0 = (p11 * row0 - p01 * row1) * scale
        lead1 = (p00 * row1 - p01 * row0) * scale
        below = work[top:, :]
        left = below - below[:, step : step + 1] * lead0 - below[:, step + 1 : step + 2] * lead1
        below = jnp.where(sub[top:, :] > step + 1, left, below)
        work = jnp.concatenate([work[:top, :], below], 0) if top else below
    above = pltpu.roll(work, 1, 0)
    lower = (lane == sub - 1) & (sub % 2 == 1)
    cross = jnp.sum(jnp.where(lower, work, 0.0), axis=1, keepdims=True)
    pivot = jnp.sum(jnp.where(lower, above, 0.0), axis=1, keepdims=True)
    odd = sub[:, :1] % 2 == 1
    work = work - jnp.where(odd, cross / jnp.where(odd, pivot, 1.0), 0.0) * above
    diagonal = jnp.sum(jnp.where(lane == sub, work, 0.0), axis=1, keepdims=True)
    return work[:, rank : 2 * rank] / jnp.sqrt(diagonal)


def fresh_left(inverse):
    h1, h2, h3 = split3(inverse)
    return jnp.concatenate([h1, h1, h2, h1, h2, h3, h2, h3], 1)


def fresh_of(left, applied):
    a1, a2, a3 = split3(applied)
    right = jnp.concatenate([a1, a2, a1, a3, a2, a1, a3, a2], 0)
    return jnp.dot(left, right, preferred_element_type=F32)


def clear_pads(ref, columns):
    for column in range(columns):
        for slot in list(range(PAD)) + list(range(SLOTS - PAD, SLOTS)):
            ref[column * SLOTS + slot] = jnp.zeros(ref.shape[1:], ref.dtype)


def turn_in(turned_ref, at, rows):
    depth = rows.shape[0]
    padded = jnp.concatenate([rows, jnp.zeros((DEPTH - depth, rows.shape[1]), F32)], 0)
    turned_ref[at] = jnp.transpose(padded).astype(BF16)
    return padded.astype(BF16)


def own_shift(listed_ref):
    middle = COLW + COLW // 2 - 1
    return -jnp.clip(listed_ref[middle, 0] - listed_ref[middle, 3] + COLW, -1, 1)


def halo_shifts(listed_ref):
    middle = COLW // 2 - 1
    before = listed_ref[middle, 0] - listed_ref[middle, 3] + COLW
    after = listed_ref[COLW + middle, 8] - listed_ref[COLW + middle, 5] - COLW
    return jnp.clip(before, -1, 1), jnp.clip(after, -1, 1)


def own_apply(blocks, iter_ref, acc_ref, home, other, across):
    left, right = iter_ref[home], iter_ref[other]
    total = times(left, blocks[0]) + times(iter_ref[home + 1], blocks[1])
    for k in range(3):
        total = total + times(iter_ref[across + k], blocks[2 + k])
    acc_ref[home] += total
    acc_ref[home + 1] += times_turned(left, blocks[1])
    for k in range(3):
        acc_ref[across + k] += times_turned(left, blocks[2 + k])
    acc_ref[other] += times(right, blocks[5]) + times(iter_ref[other + 1], blocks[6])
    acc_ref[other + 1] += times_turned(right, blocks[6])


def own_kernel(
    wet_ref, listed_ref, members_ref, initial_ref,
    table_ref, padded_ref, block_ref, part_ref,
    wide_ref, turned_ref, iter_ref,
):
    make_tapers(table_ref, wide_ref, float(members_ref.shape[1]))
    clear_pads(turned_ref, 2)
    clear_pads(iter_ref, 2)
    part_ref[...] = jnp.zeros_like(part_ref)

    @pl.loop(0, 2 * COLW)
    def _(tile):
        at = tile + PAD + jnp.where(tile >= COLW, 2 * PAD, 0)
        lane = lax.broadcasted_iota(jnp.int32, members_ref.shape[1:], 1)
        rows = jnp.where(lane < wet_ref[tile], members_ref[tile].astype(F32), 0.0)
        padded_ref[tile] = turn_in(turned_ref, at, rows)
        iter_ref[at] = initial_ref[tile]

    moved = own_shift(listed_ref)
    same, next_up = table_ref.at[4], table_ref.at[5]

    @pl.loop(0, COLW)
    def _(r):
        home = PAD + r
        other = SLOTS + PAD + r
        across = other + moved - 1
        blocks = block_ref.at[r]
        left = padded_ref[r]
        make_blocks(turned_ref, home, left, (same, next_up), blocks, 0)
        make_blocks(turned_ref, across, left, [table_ref.at[6 + k] for k in range(3)], blocks, 2)
        make_blocks(turned_ref, other, padded_ref[COLW + r], (same, next_up), blocks, 5)
        own_apply(blocks, iter_ref, part_ref, home, other, across)


def halo_kernel(
    listed_ref, padded_ref, table_ref, part_ref, left_ref, right_ref,
    block_ref, first_ref, second_ref, gram_out_ref,
    turned_ref, iter_ref, last_ref, gram_ref,
):
    rank = iter_ref.shape[1]
    count = left_ref.shape[1] - rank
    clear_pads(turned_ref, 2)
    clear_pads(iter_ref, 2)
    gram_ref[...] = jnp.zeros_like(gram_ref)
    last_ref[...] = jnp.zeros_like(last_ref)

    @pl.loop(0, COLW)
    def _(tile):
        for column, ref in enumerate((left_ref, right_ref)):
            at = column * SLOTS + PAD + tile
            turn_in(turned_ref, at, ref[tile, :count, :].astype(F32))
            iter_ref[at] = ref[tile, count:, :]

    shifts = halo_shifts(listed_ref)

    @pl.loop(0, COLW)
    def _(r):
        for column in range(2):
            at = column * SLOTS + PAD + r + shifts[column] - 1
            make_blocks(
                turned_ref, at, padded_ref[column * COLW + r],
                [table_ref.at[6 * column + k] for k in range(3)], block_ref.at[r], column * 3,
            )
        for column in range(2):
            at = column * SLOTS + PAD + r + shifts[column] - 1
            total = part_ref[column * SLOTS + PAD + r]
            for k in range(3):
                total = total + times(iter_ref[at + k], block_ref[r, column * 3 + k])
            (first_ref, second_ref)[column][r] = total
            gram_add(gram_ref, last_ref[column])
            last_ref[column] = total

    for column in range(2):
        gram_add(gram_ref, last_ref[column])
    gram_out_ref[...] = jnp.broadcast_to(gram_packed(gram_ref, rank)[None], gram_out_ref.shape)


def again_kernel(
    total_points,
    listed_ref, grams_ref, first_ref, second_ref, left_ref, right_ref, own_ref, halo_ref,
    out_ref, gram_out_ref,
    iter_ref, acc_ref, gram_ref,
):
    rank = first_ref.shape[1]

    clear_pads(iter_ref, 4)
    gram_ref[...] = jnp.zeros_like(gram_ref)
    left = fresh_left(inverse_factor(jnp.sum(grams_ref[...], 0), rank, total_points))

    @pl.loop(0, COLW)
    def _(r):
        for column, ref in enumerate((left_ref, first_ref, second_ref, right_ref)):
            iter_ref[column * SLOTS + PAD + r] = fresh_of(left, ref[r]).astype(BF16)

    acc_ref[...] = jnp.zeros_like(acc_ref)
    moved = own_shift(listed_ref)
    shifts = halo_shifts(listed_ref)

    @pl.loop(0, COLW)
    def _(r):
        home = SLOTS + PAD + r
        own_apply(own_ref.at[r], iter_ref, acc_ref, home, home + SLOTS, home + SLOTS + moved - 1)
        for column in range(2):
            at = column * 3 * SLOTS + PAD + r + shifts[column] - 1
            total = times(iter_ref[at], halo_ref[r, column * 3])
            for k in range(1, 3):
                total = total + times(iter_ref[at + k], halo_ref[r, column * 3 + k])
            acc_ref[home + column * SLOTS] += total

    @pl.loop(0, COLW)
    def _(r):
        for column in range(2):
            total = acc_ref[(column + 1) * SLOTS + PAD + r]
            out_ref[column * COLW + r] = total
            gram_add(gram_ref, total)

    gram_out_ref[...] = jnp.broadcast_to(gram_packed(gram_ref, rank)[None], gram_out_ref.shape)


def last_kernel(total_points, grams_ref, applied_ref, out_ref):
    rank = applied_ref.shape[1]
    left = fresh_left(inverse_factor(jnp.sum(grams_ref[...], 0), rank, total_points))

    @pl.loop(0, applied_ref.shape[0])
    def _(tile):
        out_ref[tile] = fresh_of(left, applied_ref[tile])


def fold_kernel(in_ref, out_ref):
    out_ref[...] = jnp.broadcast_to(jnp.sum(in_ref[...], 0)[None], out_ref.shape)


def cost(flops, moved):
    return pl.CostEstimate(flops=flops, bytes_accessed=moved, transcendentals=0)


SMEM = pl.BlockSpec(memory_space=pltpu.SMEM)
VMEM = pl.BlockSpec(memory_space=pltpu.VMEM)
PARAMS = pltpu.CompilerParams(vmem_limit_bytes=VMEM_LIMIT)
SMALL = pltpu.CompilerParams(vmem_limit_bytes=4 * 1024 * 1024)


def shifted(shard, by):
    length = lax.axis_size(TILES_REP)
    pairs = [(i, i + by) for i in range(length) if 0 <= i + by < length]
    return lax.ppermute(shard, TILES_REP, pairs)


def exchanged(shard, axes):
    return lax.all_to_all(shard, axes, split_axis=0, concat_axis=0, tiled=True)


def gathered(copies):
    line = lax.axis_size(LINE)
    plane = exchanged(copies, PLANE)
    summed = pl.pallas_call(
        fold_kernel,
        out_shape=jax.ShapeDtypeStruct((line, *copies.shape[1:]), F32),
        in_specs=[VMEM],
        out_specs=VMEM,
        compiler_params=SMALL,
        name="fold",
    )(plane)
    return exchanged(summed, LINE)


def local(members, initial, wet_counts, tile_coords, neighbours):
    tiles, count, points = members.shape
    rank = initial.shape[1]
    assert tiles == 2 * COLW and points == SIDE * SIDE and rank == 32
    shape = jax.ShapeDtypeStruct
    total_points = float(tiles * lax.axis_size(TILES_REP) * points)
    plane = lax.axis_size(PLANE)
    packed = (8, rank * rank // 8)

    lane = jnp.arange(points, dtype=jnp.int32)
    masked = jnp.where((lane[None, :] < wet_counts[:, None])[:, None, :], members, jnp.zeros_like(members))
    from_right = shifted(jnp.concatenate([masked[:COLW], initial[:COLW]], 1), -1)
    from_left = shifted(jnp.concatenate([masked[COLW:], initial[COLW:]], 1), 1)

    table_s, padded_s = shape((9, points, points), F32), shape((tiles, DEPTH, points), BF16)
    own_s, part_s = shape((COLW, 7, points, points), BF16), shape((2 * SLOTS, rank, points), F32)
    halo_s, half_s = shape((COLW, 6, points, points), BF16), shape((COLW, rank, points), F32)
    turned_s = pltpu.VMEM((2 * SLOTS, points, DEPTH), BF16)
    table, padded, own_blocks, part = pl.pallas_call(
        own_kernel,
        out_shape=(table_s, padded_s, own_s, part_s),
        in_specs=[SMEM, SMEM, VMEM, VMEM],
        out_specs=(VMEM,) * 4,
        scratch_shapes=[
            pltpu.VMEM((3, SIDE, 64 * SIDE), F32),
            turned_s,
            pltpu.VMEM((2 * SLOTS, rank, points), BF16),
        ],
        compiler_params=PARAMS,
        cost_estimate=cost(96 * 2 * points * points * (DEPTH + rank), 40_000_000),
        name="own_blocks",
    )(wet_counts, neighbours, members, initial)

    halo_blocks, first, second, copies = pl.pallas_call(
        halo_kernel,
        out_shape=(halo_s, half_s, half_s, shape((plane, *packed), F32)),
        in_specs=[SMEM] + [VMEM] * 5,
        out_specs=(VMEM,) * 4,
        scratch_shapes=[
            turned_s,
            pltpu.VMEM((2 * SLOTS, rank, points), BF16),
            pltpu.VMEM((2, rank, points), F32),
            pltpu.VMEM((3 * rank, 3 * rank), F32),
        ],
        compiler_params=PARAMS,
        cost_estimate=cost(48 * 2 * points * points * (DEPTH + rank), 20_000_000),
        name="halo_blocks",
    )(neighbours, padded, table, part, from_left, from_right)

    after = shifted(first, -1)
    before = shifted(second, 1)
    applied, copies = pl.pallas_call(
        functools.partial(again_kernel, total_points),
        out_shape=(shape((tiles, rank, points), F32), shape((plane, *packed), F32)),
        in_specs=[SMEM] + [VMEM] * 7,
        out_specs=(VMEM, VMEM),
        scratch_shapes=[
            pltpu.VMEM((4 * SLOTS, rank, points), BF16),
            pltpu.VMEM((4 * SLOTS, rank, points), F32),
            pltpu.VMEM((3 * rank, 3 * rank), F32),
        ],
        compiler_params=pltpu.CompilerParams(vmem_limit_bytes=24 * 1024 * 1024),
        name="apply_again",
    )(neighbours, gathered(copies), first, second, before, after, own_blocks, halo_blocks)

    return pl.pallas_call(
        functools.partial(last_kernel, total_points),
        out_shape=shape((tiles, rank, points), F32),
        in_specs=[VMEM, VMEM],
        out_specs=VMEM,
        compiler_params=SMALL,
        name="last_fresh",
    )(gathered(copies), applied)


def solution(mesh):
    split = Mesh(mesh.devices.reshape(*SPLIT, mesh.shape["rep"]), TILES_REP)
    return jax.shard_map(
        local,
        mesh=split,
        in_specs=(
            P(TILES_REP, None, None),
            P(TILES_REP, None, None),
            P(TILES_REP),
            P(TILES_REP, None),
            P(TILES_REP, None),
        ),
        out_specs=P(TILES_REP, None, None),
        check_vma=False,
    )
```

```python
import functools

import jax
import jax.numpy as jnp
from jax import lax
from jax.experimental import pallas as pl
from jax.experimental.pallas import tpu as pltpu
from jax.sharding import Mesh
from jax.sharding import PartitionSpec as P

SIDE = 16
COLW = 8
SPLIT = (4, 16, 4)
TILES_REP = ("tiles_0", "tiles_1", "tiles_2", "rep")
PLANE = ("tiles_0", "tiles_2", "rep")
LINE = ("tiles_1",)
PAD = 2
SLOTS = COLW + 2 * PAD
DEPTH = 128
F32 = jnp.float32
BF16 = jnp.bfloat16
VMEM_LIMIT = 20 * 1024 * 1024


def gaspari(scaled):
    clamped = jnp.maximum(scaled, 1.0)
    inner = (((-0.25 * scaled + 0.5) * scaled + 0.625) * scaled - 5.0 / 3.0) * scaled * scaled + 1.0
    outer = (
        ((((scaled / 12.0 - 0.5) * scaled + 0.625) * scaled + 5.0 / 3.0) * scaled - 5.0) * scaled
        + 4.0
        - 2.0 / (3.0 * clamped)
    )
    return jnp.where(scaled <= 1.0, inner, jnp.where(scaled <= 2.0, outer, 0.0))


def make_tapers(table_ref, wide_ref, members):
    shape = (SIDE, 64 * SIDE)
    lane = lax.broadcasted_iota(jnp.int32, shape, 1)
    sub = lax.broadcasted_iota(jnp.int32, shape, 0)
    apart_row = (2 * SIDE - 1 - lane // SIDE).astype(F32)
    for k in range(3):
        apart_col = (SIDE * (k - 1) + sub - lane % SIDE).astype(F32)
        distance = jnp.sqrt(apart_row * apart_row + apart_col * apart_col)
        wide_ref[k] = gaspari(distance / (0.5 * SIDE)) / (members - 1.0)
    per_group = 128 // SIDE
    for k in range(3):
        wide = wide_ref[k]
        for turn in range(per_group):
            rolled = pltpu.roll(wide, 64 * SIDE - turn * SIDE, 1) if turn else wide
            for d in range(3):
                for row in range(SIDE):
                    first = 2 * SIDE - 1 - SIDE * (d - 1) - row
                    if first % per_group == turn:
                        start = (first - turn) * SIDE
                        table_ref[d * 3 + k, row * SIDE : (row + 1) * SIDE, :] = rolled[
                            :, start : start + SIDE * SIDE
                        ]


def split3(x):
    high = x.astype(BF16)
    rest = x - high.astype(F32)
    mid = rest.astype(BF16)
    low = (rest - mid.astype(F32)).astype(BF16)
    return high, mid, low


def make_blocks(turned_ref, at, right, tables, block_ref, first):
    points = right.shape[1]
    count = len(tables)
    for n, table in enumerate(tables):
        product = jnp.dot(turned_ref[at + n], right, preferred_element_type=F32)
        block_ref[first + n] = (product * table[...]).astype(BF16)


def times(rows, block):
    return jnp.dot(rows, block, preferred_element_type=F32)


def times_turned(rows, block):
    return lax.dot_general(rows, block, (((1,), (1,)), ((), ())), preferred_element_type=F32)


def gram_add(gram_ref, applied):
    parts = jnp.concatenate(split3(applied), 0)
    gram_ref[...] += lax.dot_general(parts, parts, (((1,), (1,)), ((), ())), preferred_element_type=F32)


def gram_packed(gram_ref, rank):
    full = gram_ref[...]

    def piece(a, b):
        return full[a * rank : (a + 1) * rank, b * rank : (b + 1) * rank]

    small = piece(0, 2) + piece(2, 0) + piece(1, 1) + (piece(1, 2) + piece(2, 1))
    total = piece(0, 0) + (piece(0, 1) + piece(1, 0) + small)
    return jnp.concatenate([total[8 * q : 8 * q + 8, :] for q in range(rank // 8)], 1)


def inverse_factor(packed, rank, total_points):
    gram = jnp.concatenate([packed[:, rank * q : rank * (q + 1)] for q in range(rank // 8)], 0)
    gram = gram / total_points
    work = jnp.concatenate([gram, jnp.zeros((rank, 128 - rank), F32)], 1)
    lane = lax.broadcasted_iota(jnp.int32, (rank, 128), 1)
    sub = lax.broadcasted_iota(jnp.int32, (rank, 128), 0)
    work = jnp.where(lane == sub + rank, 1.0, work)
    for step in range(0, rank - 2, 2):
        top = (step + 2) // 8 * 8
        row0, row1 = work[step : step + 1, :], work[step + 1 : step + 2, :]
        p00, p01 = row0[:, step : step + 1], row0[:, step + 1 : step + 2]
        p11 = row1[:, step + 1 : step + 2]
        scale = 1.0 / (p00 * p11 - p01 * p01)
        lead0 = (p11 * row0 - p01 * row1) * scale
        lead1 = (p00 * row1 - p01 * row0) * scale
        below = work[top:, :]
        left = below - below[:, step : step + 1] * lead0 - below[:, step + 1 : step + 2] * lead1
        below = jnp.where(sub[top:, :] > step + 1, left, below)
        work = jnp.concatenate([work[:top, :], below], 0) if top else below
    above = pltpu.roll(work, 1, 0)
    lower = (lane == sub - 1) & (sub % 2 == 1)
    cross = jnp.sum(jnp.where(lower, work, 0.0), axis=1, keepdims=True)
    pivot = jnp.sum(jnp.where(lower, above, 0.0), axis=1, keepdims=True)
    odd = sub[:, :1] % 2 == 1
    work = work - jnp.where(odd, cross / jnp.where(odd, pivot, 1.0), 0.0) * above
    diagonal = jnp.sum(jnp.where(lane == sub, work, 0.0), axis=1, keepdims=True)
    return work[:, rank : 2 * rank] / jnp.sqrt(diagonal)


def fresh_left(inverse):
    h1, h2, h3 = split3(inverse)
    return jnp.concatenate([h1, h1, h2, h1, h2, h3, h2, h3], 1)


def fresh_of(left, applied):
    a1, a2, a3 = split3(applied)
    right = jnp.concatenate([a1, a2, a1, a3, a2, a1, a3, a2], 0)
    return jnp.dot(left, right, preferred_element_type=F32)


def clear_pads(ref, columns):
    for column in range(columns):
        for slot in list(range(PAD)) + list(range(SLOTS - PAD, SLOTS)):
            ref[column * SLOTS + slot] = jnp.zeros(ref.shape[1:], ref.dtype)


def turn_in(turned_ref, at, rows):
    depth = rows.shape[0]
    padded = jnp.concatenate([rows, jnp.zeros((DEPTH - depth, rows.shape[1]), F32)], 0)
    turned_ref[at] = jnp.transpose(padded).astype(BF16)
    return padded.astype(BF16)


def own_shift(listed_ref):
    middle = COLW + COLW // 2 - 1
    return -jnp.clip(listed_ref[middle, 0] - listed_ref[middle, 3] + COLW, -1, 1)


def halo_shifts(listed_ref):
    middle = COLW // 2 - 1
    before = listed_ref[middle, 0] - listed_ref[middle, 3] + COLW
    after = listed_ref[COLW + middle, 8] - listed_ref[COLW + middle, 5] - COLW
    return jnp.clip(before, -1, 1), jnp.clip(after, -1, 1)


def own_apply(blocks, iter_ref, acc_ref, home, other, across):
    left, right = iter_ref[home], iter_ref[other]
    total = times(left, blocks[0]) + times(iter_ref[home + 1], blocks[1])
    for k in range(3):
        total = total + times(iter_ref[across + k], blocks[2 + k])
    acc_ref[home] += total
    acc_ref[home + 1] += times_turned(left, blocks[1])
    for k in range(3):
        acc_ref[across + k] += times_turned(left, blocks[2 + k])
    acc_ref[other] += times(right, blocks[5]) + times(iter_ref[other + 1], blocks[6])
    acc_ref[other + 1] += times_turned(right, blocks[6])


def pack_kernel(wet_ref, members_ref, initial_ref, low_ref, high_ref):
    count = members_ref.shape[1]
    lane = lax.broadcasted_iota(jnp.int32, members_ref.shape[1:], 1)

    @pl.loop(0, COLW)
    def _(tile):
        for half, ref in enumerate((low_ref, high_ref)):
            at = half * COLW + tile
            rows = jnp.where(lane < wet_ref[at], members_ref[at].astype(F32), 0.0)
            ref[tile, :count, :] = rows.astype(BF16)
            ref[tile, count:, :] = initial_ref[at]


def own_kernel(
    listed_hbm, low_ref, high_ref,
    table_ref, padded_ref, block_ref, part_ref,
    wide_ref, turned_ref, iter_ref, listed_ref, sem,
):
    fetch = pltpu.make_async_copy(listed_hbm, listed_ref, sem)
    fetch.start()
    count = low_ref.shape[1] - iter_ref.shape[1]
    make_tapers(table_ref, wide_ref, float(count))
    clear_pads(turned_ref, 2)
    clear_pads(iter_ref, 2)
    part_ref[...] = jnp.zeros_like(part_ref)

    @pl.loop(0, COLW)
    def _(tile):
        for column, ref in enumerate((low_ref, high_ref)):
            at = column * SLOTS + PAD + tile
            padded_ref[column * COLW + tile] = turn_in(turned_ref, at, ref[tile, :count, :].astype(F32))
            iter_ref[at] = ref[tile, count:, :]

    fetch.wait()
    moved = own_shift(listed_ref)
    same, next_up = table_ref.at[4], table_ref.at[5]

    @pl.loop(0, COLW)
    def _(r):
        home = PAD + r
        other = SLOTS + PAD + r
        across = other + moved - 1
        blocks = block_ref.at[r]
        left = padded_ref[r]
        make_blocks(turned_ref, home, left, (same, next_up), blocks, 0)
        make_blocks(turned_ref, across, left, [table_ref.at[6 + k] for k in range(3)], blocks, 2)
        make_blocks(turned_ref, other, padded_ref[COLW + r], (same, next_up), blocks, 5)
        own_apply(blocks, iter_ref, part_ref, home, other, across)


def halo_kernel(
    listed_hbm, padded_ref, table_ref, part_ref, left_ref, right_ref,
    block_ref, first_ref, second_ref, gram_out_ref,
    turned_ref, iter_ref, last_ref, gram_ref, listed_ref, sem,
):
    fetch = pltpu.make_async_copy(listed_hbm, listed_ref, sem)
    fetch.start()
    rank = iter_ref.shape[1]
    count = left_ref.shape[1] - rank
    clear_pads(turned_ref, 2)
    clear_pads(iter_ref, 2)
    gram_ref[...] = jnp.zeros_like(gram_ref)
    last_ref[...] = jnp.zeros_like(last_ref)

    @pl.loop(0, COLW)
    def _(tile):
        for column, ref in enumerate((left_ref, right_ref)):
            at = column * SLOTS + PAD + tile
            turn_in(turned_ref, at, ref[tile, :count, :].astype(F32))
            iter_ref[at] = ref[tile, count:, :]

    fetch.wait()
    shifts = halo_shifts(listed_ref)

    @pl.loop(0, COLW)
    def _(r):
        for column in range(2):
            at = column * SLOTS + PAD + r + shifts[column] - 1
            make_blocks(
                turned_ref, at, padded_ref[column * COLW + r],
                [table_ref.at[6 * column + k] for k in range(3)], block_ref.at[r], column * 3,
            )
        for column in range(2):
            at = column * SLOTS + PAD + r + shifts[column] - 1
            total = part_ref[column * SLOTS + PAD + r]
            for k in range(3):
                total = total + times(iter_ref[at + k], block_ref[r, column * 3 + k])
            (first_ref, second_ref)[column][r] = total
            gram_add(gram_ref, last_ref[column])
            last_ref[column] = total

    for column in range(2):
        gram_add(gram_ref, last_ref[column])
    gram_out_ref[...] = jnp.broadcast_to(gram_packed(gram_ref, rank)[None], gram_out_ref.shape)


def again_kernel(
    total_points,
    listed_hbm, grams_ref, first_ref, second_ref, left_ref, right_ref, own_ref, halo_ref,
    out_ref, gram_out_ref,
    iter_ref, acc_ref, gram_ref, listed_ref, sem,
):
    fetch = pltpu.make_async_copy(listed_hbm, listed_ref, sem)
    fetch.start()
    rank = first_ref.shape[1]

    clear_pads(iter_ref, 4)
    gram_ref[...] = jnp.zeros_like(gram_ref)
    left = fresh_left(inverse_factor(jnp.sum(grams_ref[...], 0), rank, total_points))

    @pl.loop(0, COLW)
    def _(r):
        for column, ref in enumerate((left_ref, first_ref, second_ref, right_ref)):
            iter_ref[column * SLOTS + PAD + r] = fresh_of(left, ref[r]).astype(BF16)

    acc_ref[...] = jnp.zeros_like(acc_ref)
    fetch.wait()
    moved = own_shift(listed_ref)
    shifts = halo_shifts(listed_ref)

    @pl.loop(0, COLW)
    def _(r):
        home = SLOTS + PAD + r
        own_apply(own_ref.at[r], iter_ref, acc_ref, home, home + SLOTS, home + SLOTS + moved - 1)
        for column in range(2):
            at = column * 3 * SLOTS + PAD + r + shifts[column] - 1
            total = times(iter_ref[at], halo_ref[r, column * 3])
            for k in range(1, 3):
                total = total + times(iter_ref[at + k], halo_ref[r, column * 3 + k])
            acc_ref[home + column * SLOTS] += total

    @pl.loop(0, COLW)
    def _(r):
        for column in range(2):
            total = acc_ref[(column + 1) * SLOTS + PAD + r]
            out_ref[column * COLW + r] = total
            gram_add(gram_ref, total)

    gram_out_ref[...] = jnp.broadcast_to(gram_packed(gram_ref, rank)[None], gram_out_ref.shape)


def last_kernel(total_points, grams_ref, applied_ref, out_ref):
    rank = applied_ref.shape[1]
    left = fresh_left(inverse_factor(jnp.sum(grams_ref[...], 0), rank, total_points))

    @pl.loop(0, applied_ref.shape[0])
    def _(tile):
        out_ref[tile] = fresh_of(left, applied_ref[tile])


def fold_kernel(in_ref, out_ref):
    out_ref[...] = jnp.broadcast_to(jnp.sum(in_ref[...], 0)[None], out_ref.shape)


def cost(flops, moved):
    return pl.CostEstimate(flops=flops, bytes_accessed=moved, transcendentals=0)


SMEM = pl.BlockSpec(memory_space=pltpu.SMEM)
VMEM = pl.BlockSpec(memory_space=pltpu.VMEM)
HBM = pl.BlockSpec(memory_space=pltpu.HBM)
PARAMS = pltpu.CompilerParams(vmem_limit_bytes=VMEM_LIMIT)
SMALL = pltpu.CompilerParams(vmem_limit_bytes=4 * 1024 * 1024)


def shifted(shard, by):
    length = lax.axis_size(TILES_REP)
    pairs = [(i, i + by) for i in range(length) if 0 <= i + by < length]
    return lax.ppermute(shard, TILES_REP, pairs)


def exchanged(shard, axes):
    return lax.all_to_all(shard, axes, split_axis=0, concat_axis=0, tiled=True)


def gathered(copies, *beside):
    line = lax.axis_size(LINE)
    plane, *beside = lax.optimization_barrier((exchanged(copies, PLANE), *beside))
    summed = pl.pallas_call(
        fold_kernel,
        out_shape=jax.ShapeDtypeStruct((line, *copies.shape[1:]), F32),
        in_specs=[VMEM],
        out_specs=VMEM,
        compiler_params=SMALL,
        name="fold",
    )(plane)
    return exchanged(summed, LINE), *beside


def local(members, initial, wet_counts, tile_coords, neighbours):
    tiles, count, points = members.shape
    rank = initial.shape[1]
    assert tiles == 2 * COLW and points == SIDE * SIDE and rank == 32
    shape = jax.ShapeDtypeStruct
    total_points = float(tiles * lax.axis_size(TILES_REP) * points)
    plane = lax.axis_size(PLANE)
    packed = (8, rank * rank // 8)

    members, initial, wet_counts, neighbours = (
        pltpu.with_memory_space_constraint(x, pltpu.HBM) for x in (members, initial, wet_counts, neighbours)
    )
    pair_s = shape((COLW, count + rank, points), BF16)
    low, high = pl.pallas_call(
        pack_kernel,
        out_shape=(pair_s, pair_s),
        in_specs=[SMEM, VMEM, VMEM],
        out_specs=(VMEM, VMEM),
        compiler_params=SMALL,
        name="pack",
    )(wet_counts, members, initial)
    from_right = shifted(low, -1)
    from_left = shifted(high, 1)

    table_s, padded_s = shape((9, points, points), F32), shape((tiles, DEPTH, points), BF16)
    own_s, part_s = shape((COLW, 7, points, points), BF16), shape((2 * SLOTS, rank, points), F32)
    halo_s, half_s = shape((COLW, 6, points, points), BF16), shape((COLW, rank, points), F32)
    listed_s = (pltpu.SMEM(neighbours.shape, jnp.int32), pltpu.SemaphoreType.DMA)
    turned_s = pltpu.VMEM((2 * SLOTS, points, DEPTH), BF16)
    table, padded, own_blocks, part = pl.pallas_call(
        own_kernel,
        out_shape=(table_s, padded_s, own_s, part_s),
        in_specs=[HBM, VMEM, VMEM],
        out_specs=(VMEM,) * 4,
        scratch_shapes=[
            pltpu.VMEM((3, SIDE, 64 * SIDE), F32),
            turned_s,
            pltpu.VMEM((2 * SLOTS, rank, points), BF16),
            *listed_s,
        ],
        compiler_params=PARAMS,
        cost_estimate=cost(96 * 2 * points * points * (DEPTH + rank), 40_000_000),
        name="own_blocks",
    )(neighbours, low, high)

    halo_blocks, first, second, copies = pl.pallas_call(
        halo_kernel,
        out_shape=(halo_s, half_s, half_s, shape((plane, *packed), F32)),
        in_specs=[HBM] + [VMEM] * 5,
        out_specs=(VMEM,) * 4,
        scratch_shapes=[
            turned_s,
            pltpu.VMEM((2 * SLOTS, rank, points), BF16),
            pltpu.VMEM((2, rank, points), F32),
            pltpu.VMEM((3 * rank, 3 * rank), F32),
            *listed_s,
        ],
        compiler_params=PARAMS,
        cost_estimate=cost(48 * 2 * points * points * (DEPTH + rank), 20_000_000),
        name="halo_blocks",
    )(neighbours, padded, table, part, from_left, from_right)

    grams, after, before = gathered(copies, shifted(first, -1), shifted(second, 1))
    applied, copies = pl.pallas_call(
        functools.partial(again_kernel, total_points),
        out_shape=(shape((tiles, rank, points), F32), shape((plane, *packed), F32)),
        in_specs=[HBM] + [VMEM] * 7,
        out_specs=(VMEM, VMEM),
        scratch_shapes=[
            pltpu.VMEM((4 * SLOTS, rank, points), BF16),
            pltpu.VMEM((4 * SLOTS, rank, points), F32),
            pltpu.VMEM((3 * rank, 3 * rank), F32),
            *listed_s,
        ],
        compiler_params=pltpu.CompilerParams(vmem_limit_bytes=24 * 1024 * 1024),
        name="apply_again",
    )(neighbours, grams, first, second, before, after, own_blocks, halo_blocks)

    return pl.pallas_call(
        functools.partial(last_kernel, total_points),
        out_shape=shape((tiles, rank, points), F32),
        in_specs=[VMEM, VMEM],
        out_specs=VMEM,
        compiler_params=SMALL,
        name="last_fresh",
    )(*gathered(copies), applied)


def solution(mesh):
    split = Mesh(mesh.devices.reshape(*SPLIT, mesh.shape["rep"]), TILES_REP)
    return jax.shard_map(
        local,
        mesh=split,
        in_specs=(
            P(TILES_REP, None, None),
            P(TILES_REP, None, None),
            P(TILES_REP),
            P(TILES_REP, None),
            P(TILES_REP, None),
        ),
        out_specs=P(TILES_REP, None, None),
        check_vma=False,
    )
```

```python
import functools

import jax
import jax.numpy as jnp
from jax import lax
from jax.experimental import pallas as pl
from jax.experimental.pallas import tpu as pltpu
from jax.sharding import Mesh
from jax.sharding import PartitionSpec as P

SIDE = 16
COLW = 8
SPLIT = (4, 16, 4)
TILES_REP = ("tiles_0", "tiles_1", "tiles_2", "rep")
PLANE = ("tiles_0", "tiles_2", "rep")
LINE = ("tiles_1",)
PAD = 2
SLOTS = COLW + 2 * PAD
DEPTH = 128
F32 = jnp.float32
BF16 = jnp.bfloat16
VMEM_LIMIT = 20 * 1024 * 1024


def gaspari(scaled):
    clamped = jnp.maximum(scaled, 1.0)
    inner = (((-0.25 * scaled + 0.5) * scaled + 0.625) * scaled - 5.0 / 3.0) * scaled * scaled + 1.0
    outer = (
        ((((scaled / 12.0 - 0.5) * scaled + 0.625) * scaled + 5.0 / 3.0) * scaled - 5.0) * scaled
        + 4.0
        - 2.0 / (3.0 * clamped)
    )
    return jnp.where(scaled <= 1.0, inner, jnp.where(scaled <= 2.0, outer, 0.0))


def make_tapers(table_ref, wide_ref, members):
    shape = (SIDE, 64 * SIDE)
    lane = lax.broadcasted_iota(jnp.int32, shape, 1)
    sub = lax.broadcasted_iota(jnp.int32, shape, 0)
    apart_row = (2 * SIDE - 1 - lane // SIDE).astype(F32)
    for k in range(3):
        apart_col = (SIDE * (k - 1) + sub - lane % SIDE).astype(F32)
        distance = jnp.sqrt(apart_row * apart_row + apart_col * apart_col)
        wide_ref[k] = gaspari(distance / (0.5 * SIDE)) / (members - 1.0)
    per_group = 128 // SIDE
    for k in range(3):
        wide = wide_ref[k]
        for turn in range(per_group):
            rolled = pltpu.roll(wide, 64 * SIDE - turn * SIDE, 1) if turn else wide
            for d in range(3):
                for row in range(SIDE):
                    first = 2 * SIDE - 1 - SIDE * (d - 1) - row
                    if first % per_group == turn:
                        start = (first - turn) * SIDE
                        table_ref[d * 3 + k, row * SIDE : (row + 1) * SIDE, :] = rolled[
                            :, start : start + SIDE * SIDE
                        ]


def split3(x):
    high = x.astype(BF16)
    rest = x - high.astype(F32)
    mid = rest.astype(BF16)
    low = (rest - mid.astype(F32)).astype(BF16)
    return high, mid, low


def make_blocks(turned_ref, at, right, tables, block_ref, first):
    points = right.shape[1]
    count = len(tables)
    for n, table in enumerate(tables):
        product = jnp.dot(turned_ref[at + n], right, preferred_element_type=F32)
        block_ref[first + n] = (product * table[...]).astype(BF16)


def times(rows, block):
    return jnp.dot(rows, block, preferred_element_type=F32)


def times_turned(rows, block):
    return lax.dot_general(rows, block, (((1,), (1,)), ((), ())), preferred_element_type=F32)


def gram_add(gram_ref, applied):
    parts = jnp.concatenate(split3(applied), 0)
    gram_ref[...] += lax.dot_general(parts, parts, (((1,), (1,)), ((), ())), preferred_element_type=F32)


def gram_packed(gram_ref, rank):
    full = gram_ref[...]

    def piece(a, b):
        return full[a * rank : (a + 1) * rank, b * rank : (b + 1) * rank]

    small = piece(0, 2) + piece(2, 0) + piece(1, 1) + (piece(1, 2) + piece(2, 1))
    total = piece(0, 0) + (piece(0, 1) + piece(1, 0) + small)
    return jnp.concatenate([total[8 * q : 8 * q + 8, :] for q in range(rank // 8)], 1)


def inverse_factor(packed, rank, total_points):
    gram = jnp.concatenate([packed[:, rank * q : rank * (q + 1)] for q in range(rank // 8)], 0)
    gram = gram / total_points
    work = jnp.concatenate([gram, jnp.zeros((rank, 128 - rank), F32)], 1)
    lane = lax.broadcasted_iota(jnp.int32, (rank, 128), 1)
    sub = lax.broadcasted_iota(jnp.int32, (rank, 128), 0)
    work = jnp.where(lane == sub + rank, 1.0, work)
    groups = []
    for step in range(0, rank, 4):
        base = step // 8 * 8
        at = step - base
        below = work[base:, :]
        columns = [jnp.broadcast_to(below[:, step + j : step + j + 1], below.shape) for j in range(4)]

        def pivot(i, j):
            return columns[j][at + i : at + i + 1, :]

        r0, r1, r2, r3 = (below[at + i : at + i + 1, :] for i in range(4))
        a00, a10, a11 = pivot(0, 0), pivot(1, 0), pivot(1, 1)
        over = 1.0 / (a00 * a11 - a10 * a10)
        i00, i10, i11 = a11 * over, -a10 * over, a00 * over
        b00, b01, b10, b11 = pivot(2, 0), pivot(2, 1), pivot(3, 0), pivot(3, 1)
        y00, y01 = b00 * i00 + b01 * i10, b00 * i10 + b01 * i11
        y10, y11 = b10 * i00 + b11 * i10, b10 * i10 + b11 * i11
        s00 = pivot(2, 2) - (y00 * b00 + y01 * b01)
        s10 = pivot(3, 2) - (y10 * b00 + y11 * b01)
        s11 = pivot(3, 3) - (y10 * b10 + y11 * b11)
        w2 = r2 - (y00 * r0 + y01 * r1)
        w3 = r3 - (y10 * r0 + y11 * r1)
        q1, q3 = a10 / a00, s10 / s00
        done = (
            r0 / jnp.sqrt(a00),
            (r1 - q1 * r0) / jnp.sqrt(a11 - q1 * a10),
            w2 / jnp.sqrt(s00),
            (w3 - q3 * w2) / jnp.sqrt(s11 - q3 * s10),
        )
        if at == 0:
            groups.append(jnp.zeros((8, 128), F32))
        for i in range(4):
            groups[-1] = jnp.where(sub[:8, :] == at + i, done[i], groups[-1])
        if step + 4 < rank:
            over = 1.0 / (s00 * s11 - s10 * s10)
            z2 = (s11 * w2 - s10 * w3) * over
            z3 = (s00 * w3 - s10 * w2) * over
            z0 = i00 * r0 + i10 * r1 - (y00 * z2 + y10 * z3)
            z1 = i10 * r0 + i11 * r1 - (y01 * z2 + y11 * z3)
            left = below - (columns[0] * z0 + columns[1] * z1) - (columns[2] * z2 + columns[3] * z3)
            if at == 0:
                left = jnp.where(sub[base:, :] > step + 3, left, below)
            work = jnp.concatenate([work[:base, :], left], 0) if base else left
    return jnp.concatenate(groups, 0)[:, rank : 2 * rank]


def fresh_left(inverse):
    h1, h2, h3 = split3(inverse)
    return jnp.concatenate([h1, h1, h2, h1, h2, h3, h2, h3], 1)


def fresh_of(left, applied):
    a1, a2, a3 = split3(applied)
    right = jnp.concatenate([a1, a2, a1, a3, a2, a1, a3, a2], 0)
    return jnp.dot(left, right, preferred_element_type=F32)


def clear_pads(ref, columns):
    for column in range(columns):
        for slot in list(range(PAD)) + list(range(SLOTS - PAD, SLOTS)):
            ref[column * SLOTS + slot] = jnp.zeros(ref.shape[1:], ref.dtype)


def turn_in(turned_ref, at, rows):
    depth = rows.shape[0]
    padded = jnp.concatenate([rows, jnp.zeros((DEPTH - depth, rows.shape[1]), F32)], 0)
    turned_ref[at] = jnp.transpose(padded).astype(BF16)
    return padded.astype(BF16)


def own_shift(listed_ref):
    middle = COLW + COLW // 2 - 1
    return -jnp.clip(listed_ref[middle, 0] - listed_ref[middle, 3] + COLW, -1, 1)


def halo_shifts(listed_ref):
    middle = COLW // 2 - 1
    before = listed_ref[middle, 0] - listed_ref[middle, 3] + COLW
    after = listed_ref[COLW + middle, 8] - listed_ref[COLW + middle, 5] - COLW
    return jnp.clip(before, -1, 1), jnp.clip(after, -1, 1)


def own_apply(blocks, iter_ref, acc_ref, home, other, across):
    left, right = iter_ref[home], iter_ref[other]
    total = times(left, blocks[0]) + times(iter_ref[home + 1], blocks[1])
    for k in range(3):
        total = total + times(iter_ref[across + k], blocks[2 + k])
    acc_ref[home] += total
    acc_ref[home + 1] += times_turned(left, blocks[1])
    for k in range(3):
        acc_ref[across + k] += times_turned(left, blocks[2 + k])
    acc_ref[other] += times(right, blocks[5]) + times(iter_ref[other + 1], blocks[6])
    acc_ref[other + 1] += times_turned(right, blocks[6])


def pack_kernel(wet_ref, members_ref, initial_ref, low_ref, high_ref):
    count = members_ref.shape[1]
    lane = lax.broadcasted_iota(jnp.int32, members_ref.shape[1:], 1)

    @pl.loop(0, COLW)
    def _(tile):
        for half, ref in enumerate((low_ref, high_ref)):
            at = half * COLW + tile
            rows = jnp.where(lane < wet_ref[at], members_ref[at].astype(F32), 0.0)
            ref[tile, :count, :] = rows.astype(BF16)
            ref[tile, count:, :] = initial_ref[at]


def own_kernel(
    listed_hbm, low_ref, high_ref,
    table_ref, padded_ref, block_ref, part_ref,
    wide_ref, turned_ref, iter_ref, listed_ref, sem,
):
    fetch = pltpu.make_async_copy(listed_hbm, listed_ref, sem)
    fetch.start()
    count = low_ref.shape[1] - iter_ref.shape[1]
    make_tapers(table_ref, wide_ref, float(count))
    clear_pads(turned_ref, 2)
    clear_pads(iter_ref, 2)
    part_ref[...] = jnp.zeros_like(part_ref)

    @pl.loop(0, COLW, unroll=4)
    def _(tile):
        for column, ref in enumerate((low_ref, high_ref)):
            at = column * SLOTS + PAD + tile
            padded_ref[column * COLW + tile] = turn_in(turned_ref, at, ref[tile, :count, :].astype(F32))
            iter_ref[at] = ref[tile, count:, :]

    fetch.wait()
    moved = own_shift(listed_ref)
    same, next_up = table_ref.at[4], table_ref.at[5]

    @pl.loop(0, COLW, unroll=2)
    def _(r):
        home = PAD + r
        other = SLOTS + PAD + r
        across = other + moved - 1
        blocks = block_ref.at[r]
        left = padded_ref[r]
        make_blocks(turned_ref, home, left, (same, next_up), blocks, 0)
        make_blocks(turned_ref, across, left, [table_ref.at[6 + k] for k in range(3)], blocks, 2)
        make_blocks(turned_ref, other, padded_ref[COLW + r], (same, next_up), blocks, 5)
        own_apply(blocks, iter_ref, part_ref, home, other, across)


def halo_kernel(
    listed_hbm, padded_ref, table_ref, part_ref, left_ref, right_ref,
    block_ref, first_ref, second_ref, gram_out_ref,
    turned_ref, iter_ref, last_ref, gram_ref, listed_ref, sem,
):
    fetch = pltpu.make_async_copy(listed_hbm, listed_ref, sem)
    fetch.start()
    rank = iter_ref.shape[1]
    count = left_ref.shape[1] - rank
    clear_pads(turned_ref, 2)
    clear_pads(iter_ref, 2)
    gram_ref[...] = jnp.zeros_like(gram_ref)
    last_ref[...] = jnp.zeros_like(last_ref)

    @pl.loop(0, COLW, unroll=4)
    def _(tile):
        for column, ref in enumerate((left_ref, right_ref)):
            at = column * SLOTS + PAD + tile
            turn_in(turned_ref, at, ref[tile, :count, :].astype(F32))
            iter_ref[at] = ref[tile, count:, :]

    fetch.wait()
    shifts = halo_shifts(listed_ref)

    @pl.loop(0, COLW, unroll=2)
    def _(r):
        for column in range(2):
            at = column * SLOTS + PAD + r + shifts[column] - 1
            make_blocks(
                turned_ref, at, padded_ref[column * COLW + r],
                [table_ref.at[6 * column + k] for k in range(3)], block_ref.at[r], column * 3,
            )
        for column in range(2):
            at = column * SLOTS + PAD + r + shifts[column] - 1
            total = part_ref[column * SLOTS + PAD + r]
            for k in range(3):
                total = total + times(iter_ref[at + k], block_ref[r, column * 3 + k])
            (first_ref, second_ref)[column][r] = total
            gram_add(gram_ref, last_ref[column])
            last_ref[column] = total

    for column in range(2):
        gram_add(gram_ref, last_ref[column])
    gram_out_ref[...] = jnp.broadcast_to(gram_packed(gram_ref, rank)[None], gram_out_ref.shape)


def again_kernel(
    total_points,
    listed_hbm, grams_ref, first_ref, second_ref, left_ref, right_ref, own_ref, halo_ref,
    out_ref, gram_out_ref,
    iter_ref, acc_ref, gram_ref, listed_ref, sem,
):
    fetch = pltpu.make_async_copy(listed_hbm, listed_ref, sem)
    fetch.start()
    rank = first_ref.shape[1]

    clear_pads(iter_ref, 4)
    gram_ref[...] = jnp.zeros_like(gram_ref)
    left = fresh_left(inverse_factor(jnp.sum(grams_ref[...], 0), rank, total_points))

    @pl.loop(0, COLW, unroll=4)
    def _(r):
        for column, ref in enumerate((left_ref, first_ref, second_ref, right_ref)):
            iter_ref[column * SLOTS + PAD + r] = fresh_of(left, ref[r]).astype(BF16)

    acc_ref[...] = jnp.zeros_like(acc_ref)
    fetch.wait()
    moved = own_shift(listed_ref)
    shifts = halo_shifts(listed_ref)

    @pl.loop(0, COLW, unroll=2)
    def _(r):
        home = SLOTS + PAD + r
        own_apply(own_ref.at[r], iter_ref, acc_ref, home, home + SLOTS, home + SLOTS + moved - 1)
        for column in range(2):
            at = column * 3 * SLOTS + PAD + r + shifts[column] - 1
            total = times(iter_ref[at], halo_ref[r, column * 3])
            for k in range(1, 3):
                total = total + times(iter_ref[at + k], halo_ref[r, column * 3 + k])
            acc_ref[home + column * SLOTS] += total

    @pl.loop(0, COLW, unroll=8)
    def _(r):
        for column in range(2):
            total = acc_ref[(column + 1) * SLOTS + PAD + r]
            out_ref[column * COLW + r] = total
            gram_add(gram_ref, total)

    gram_out_ref[...] = jnp.broadcast_to(gram_packed(gram_ref, rank)[None], gram_out_ref.shape)


def last_kernel(total_points, grams_ref, applied_ref, out_hbm, out_ref, sem):
    tiles, rank = applied_ref.shape[:2]
    left = fresh_left(inverse_factor(jnp.sum(grams_ref[...], 0), rank, total_points))
    share = tiles // sem.shape[0]
    sends = []
    for part in range(sem.shape[0]):
        rows = pl.ds(part * share, share)
        for tile in range(part * share, (part + 1) * share):
            out_ref[tile] = fresh_of(left, applied_ref[tile])
        sends.append(pltpu.make_async_copy(out_ref.at[rows], out_hbm.at[rows], sem.at[part]))
        sends[-1].start()
    for send in sends:
        send.wait()


def fold_kernel(in_ref, out_ref):
    out_ref[...] = jnp.broadcast_to(jnp.sum(in_ref[...], 0)[None], out_ref.shape)


def cost(flops, moved):
    return pl.CostEstimate(flops=flops, bytes_accessed=moved, transcendentals=0)


SMEM = pl.BlockSpec(memory_space=pltpu.SMEM)
VMEM = pl.BlockSpec(memory_space=pltpu.VMEM)
HBM = pl.BlockSpec(memory_space=pltpu.HBM)
PARAMS = pltpu.CompilerParams(vmem_limit_bytes=VMEM_LIMIT)
SMALL = pltpu.CompilerParams(vmem_limit_bytes=4 * 1024 * 1024)


def shifted(shard, by):
    length = lax.axis_size(TILES_REP)
    pairs = [(i, i + by) for i in range(length) if 0 <= i + by < length]
    return lax.ppermute(shard, TILES_REP, pairs)


def exchanged(shard, axes):
    return lax.all_to_all(shard, axes, split_axis=0, concat_axis=0, tiled=True)


def gathered(copies, *beside):
    line = lax.axis_size(LINE)
    plane, *beside = lax.optimization_barrier((exchanged(copies, PLANE), *beside))
    summed = pl.pallas_call(
        fold_kernel,
        out_shape=jax.ShapeDtypeStruct((line, *copies.shape[1:]), F32),
        in_specs=[VMEM],
        out_specs=VMEM,
        compiler_params=SMALL,
        name="fold",
    )(plane)
    return exchanged(summed, LINE), *beside


def local(members, initial, wet_counts, tile_coords, neighbours):
    tiles, count, points = members.shape
    rank = initial.shape[1]
    assert tiles == 2 * COLW and points == SIDE * SIDE and rank == 32
    shape = jax.ShapeDtypeStruct
    total_points = float(tiles * lax.axis_size(TILES_REP) * points)
    plane = lax.axis_size(PLANE)
    packed = (8, rank * rank // 8)

    members, initial, wet_counts, neighbours = (
        pltpu.with_memory_space_constraint(x, pltpu.HBM) for x in (members, initial, wet_counts, neighbours)
    )
    pair_s = shape((COLW, count + rank, points), BF16)
    low, high = pl.pallas_call(
        pack_kernel,
        out_shape=(pair_s, pair_s),
        in_specs=[SMEM, VMEM, VMEM],
        out_specs=(VMEM, VMEM),
        compiler_params=SMALL,
        name="pack",
    )(wet_counts, members, initial)
    from_right = shifted(low, -1)
    from_left = shifted(high, 1)

    table_s, padded_s = shape((9, points, points), F32), shape((tiles, DEPTH, points), BF16)
    own_s, part_s = shape((COLW, 7, points, points), BF16), shape((2 * SLOTS, rank, points), F32)
    halo_s, half_s = shape((COLW, 6, points, points), BF16), shape((COLW, rank, points), F32)
    listed_s = (pltpu.SMEM(neighbours.shape, jnp.int32), pltpu.SemaphoreType.DMA)
    turned_s = pltpu.VMEM((2 * SLOTS, points, DEPTH), BF16)
    table, padded, own_blocks, part = pl.pallas_call(
        own_kernel,
        out_shape=(table_s, padded_s, own_s, part_s),
        in_specs=[HBM, VMEM, VMEM],
        out_specs=(VMEM,) * 4,
        scratch_shapes=[
            pltpu.VMEM((3, SIDE, 64 * SIDE), F32),
            turned_s,
            pltpu.VMEM((2 * SLOTS, rank, points), BF16),
            *listed_s,
        ],
        compiler_params=PARAMS,
        cost_estimate=cost(96 * 2 * points * points * (DEPTH + rank), 40_000_000),
        name="own_blocks",
    )(neighbours, low, high)

    halo_blocks, first, second, copies = pl.pallas_call(
        halo_kernel,
        out_shape=(halo_s, half_s, half_s, shape((plane, *packed), F32)),
        in_specs=[HBM] + [VMEM] * 5,
        out_specs=(VMEM,) * 4,
        scratch_shapes=[
            turned_s,
            pltpu.VMEM((2 * SLOTS, rank, points), BF16),
            pltpu.VMEM((2, rank, points), F32),
            pltpu.VMEM((3 * rank, 3 * rank), F32),
            *listed_s,
        ],
        compiler_params=PARAMS,
        cost_estimate=cost(48 * 2 * points * points * (DEPTH + rank), 20_000_000),
        name="halo_blocks",
    )(neighbours, padded, table, part, from_left, from_right)

    grams, after, before = gathered(copies, shifted(first, -1), shifted(second, 1))
    applied, copies = pl.pallas_call(
        functools.partial(again_kernel, total_points),
        out_shape=(shape((tiles, rank, points), F32), shape((plane, *packed), F32)),
        in_specs=[HBM] + [VMEM] * 7,
        out_specs=(VMEM, VMEM),
        scratch_shapes=[
            pltpu.VMEM((4 * SLOTS, rank, points), BF16),
            pltpu.VMEM((4 * SLOTS, rank, points), F32),
            pltpu.VMEM((3 * rank, 3 * rank), F32),
            *listed_s,
        ],
        compiler_params=pltpu.CompilerParams(vmem_limit_bytes=24 * 1024 * 1024),
        name="apply_again",
    )(neighbours, grams, first, second, before, after, own_blocks, halo_blocks)

    return pl.pallas_call(
        functools.partial(last_kernel, total_points),
        out_shape=shape((tiles, rank, points), F32),
        in_specs=[VMEM, VMEM],
        out_specs=HBM,
        scratch_shapes=[pltpu.VMEM((tiles, rank, points), F32), pltpu.SemaphoreType.DMA((4,))],
        compiler_params=SMALL,
        name="last_fresh",
    )(*gathered(copies), applied)


def solution(mesh):
    split = Mesh(mesh.devices.reshape(*SPLIT, mesh.shape["rep"]), TILES_REP)
    return jax.shard_map(
        local,
        mesh=split,
        in_specs=(
            P(TILES_REP, None, None),
            P(TILES_REP, None, None),
            P(TILES_REP),
            P(TILES_REP, None),
            P(TILES_REP, None),
        ),
        out_specs=P(TILES_REP, None, None),
        check_vma=False,
    )
```

```python
import functools

import jax
import jax.numpy as jnp
from jax import lax
from jax.experimental import pallas as pl
from jax.experimental.pallas import tpu as pltpu
from jax.sharding import Mesh
from jax.sharding import PartitionSpec as P

SIDE = 16
COLW = 8
SPLIT = (4, 16, 4)
TILES_REP = ("tiles_0", "tiles_1", "tiles_2", "rep")
PLANE = ("tiles_0", "tiles_2", "rep")
LINE = ("tiles_1",)
PAD = 2
SLOTS = COLW + 2 * PAD
DEPTH = 128
F32 = jnp.float32
BF16 = jnp.bfloat16
VMEM_LIMIT = 20 * 1024 * 1024


def gaspari(scaled):
    clamped = jnp.maximum(scaled, 1.0)
    inner = (((-0.25 * scaled + 0.5) * scaled + 0.625) * scaled - 5.0 / 3.0) * scaled * scaled + 1.0
    outer = (
        ((((scaled / 12.0 - 0.5) * scaled + 0.625) * scaled + 5.0 / 3.0) * scaled - 5.0) * scaled
        + 4.0
        - 2.0 / (3.0 * clamped)
    )
    return jnp.where(scaled <= 1.0, inner, jnp.where(scaled <= 2.0, outer, 0.0))


def make_tapers(table_ref, wide_ref, members):
    shape = (SIDE, 64 * SIDE)
    lane = lax.broadcasted_iota(jnp.int32, shape, 1)
    sub = lax.broadcasted_iota(jnp.int32, shape, 0)
    apart_row = (2 * SIDE - 1 - lane // SIDE).astype(F32)
    for k in range(3):
        apart_col = (SIDE * (k - 1) + sub - lane % SIDE).astype(F32)
        distance = jnp.sqrt(apart_row * apart_row + apart_col * apart_col)
        wide_ref[k] = gaspari(distance / (0.5 * SIDE)) / (members - 1.0)
    per_group = 128 // SIDE
    for k in range(3):
        wide = wide_ref[k]
        for turn in range(per_group):
            rolled = pltpu.roll(wide, 64 * SIDE - turn * SIDE, 1) if turn else wide
            for d in range(3):
                for row in range(SIDE):
                    first = 2 * SIDE - 1 - SIDE * (d - 1) - row
                    if first % per_group == turn:
                        start = (first - turn) * SIDE
                        table_ref[d * 3 + k, row * SIDE : (row + 1) * SIDE, :] = rolled[
                            :, start : start + SIDE * SIDE
                        ]


def split3(x):
    high = x.astype(BF16)
    rest = x - high.astype(F32)
    mid = rest.astype(BF16)
    low = (rest - mid.astype(F32)).astype(BF16)
    return high, mid, low


def make_blocks(turned_ref, at, right, tables, block_ref, first):
    points = right.shape[1]
    count = len(tables)
    for n, table in enumerate(tables):
        product = jnp.dot(turned_ref[at + n], right, preferred_element_type=F32)
        block_ref[first + n] = (product * table[...]).astype(BF16)


def times(rows, block):
    return jnp.dot(rows, block, preferred_element_type=F32)


def times_turned(rows, block):
    return lax.dot_general(rows, block, (((1,), (1,)), ((), ())), preferred_element_type=F32)


def gram_add(gram_ref, applied):
    parts = jnp.concatenate(split3(applied), 0)
    gram_ref[...] += lax.dot_general(parts, parts, (((1,), (1,)), ((), ())), preferred_element_type=F32)


def gram_packed(gram_ref, rank):
    full = gram_ref[...]

    def piece(a, b):
        return full[a * rank : (a + 1) * rank, b * rank : (b + 1) * rank]

    small = piece(0, 2) + piece(2, 0) + piece(1, 1) + (piece(1, 2) + piece(2, 1))
    total = piece(0, 0) + (piece(0, 1) + piece(1, 0) + small)
    return jnp.concatenate([total[8 * q : 8 * q + 8, :] for q in range(rank // 8)], 1)


def inverse_factor(packed, rank, total_points):
    gram = jnp.concatenate([packed[:, rank * q : rank * (q + 1)] for q in range(rank // 8)], 0)
    gram = gram / total_points
    work = jnp.concatenate([gram, jnp.zeros((rank, 128 - rank), F32)], 1)
    lane = lax.broadcasted_iota(jnp.int32, (rank, 128), 1)
    sub = lax.broadcasted_iota(jnp.int32, (rank, 128), 0)
    work = jnp.where(lane == sub + rank, 1.0, work)
    groups = []
    for step in range(0, rank, 4):
        base = step // 8 * 8
        at = step - base
        below = work[base:, :]
        columns = [jnp.broadcast_to(below[:, step + j : step + j + 1], below.shape) for j in range(4)]

        def pivot(i, j):
            return columns[j][at + i : at + i + 1, :]

        r0, r1, r2, r3 = (below[at + i : at + i + 1, :] for i in range(4))
        a00, a10, a11 = pivot(0, 0), pivot(1, 0), pivot(1, 1)
        over = 1.0 / (a00 * a11 - a10 * a10)
        i00, i10, i11 = a11 * over, -a10 * over, a00 * over
        b00, b01, b10, b11 = pivot(2, 0), pivot(2, 1), pivot(3, 0), pivot(3, 1)
        y00, y01 = b00 * i00 + b01 * i10, b00 * i10 + b01 * i11
        y10, y11 = b10 * i00 + b11 * i10, b10 * i10 + b11 * i11
        s00 = pivot(2, 2) - (y00 * b00 + y01 * b01)
        s10 = pivot(3, 2) - (y10 * b00 + y11 * b01)
        s11 = pivot(3, 3) - (y10 * b10 + y11 * b11)
        w2 = r2 - (y00 * r0 + y01 * r1)
        w3 = r3 - (y10 * r0 + y11 * r1)
        q1, q3 = a10 / a00, s10 / s00
        done = (
            r0 / jnp.sqrt(a00),
            (r1 - q1 * r0) / jnp.sqrt(a11 - q1 * a10),
            w2 / jnp.sqrt(s00),
            (w3 - q3 * w2) / jnp.sqrt(s11 - q3 * s10),
        )
        if at == 0:
            groups.append(jnp.zeros((8, 128), F32))
        for i in range(4):
            groups[-1] = jnp.where(sub[:8, :] == at + i, done[i], groups[-1])
        if step + 4 < rank:
            over = 1.0 / (s00 * s11 - s10 * s10)
            z2 = (s11 * w2 - s10 * w3) * over
            z3 = (s00 * w3 - s10 * w2) * over
            z0 = i00 * r0 + i10 * r1 - (y00 * z2 + y10 * z3)
            z1 = i10 * r0 + i11 * r1 - (y01 * z2 + y11 * z3)
            left = below - (columns[0] * z0 + columns[1] * z1) - (columns[2] * z2 + columns[3] * z3)
            if at == 0:
                left = jnp.where(sub[base:, :] > step + 3, left, below)
            work = jnp.concatenate([work[:base, :], left], 0) if base else left
    return jnp.concatenate(groups, 0)[:, rank : 2 * rank]


def fresh_left(inverse):
    h1, h2, h3 = split3(inverse)
    return jnp.concatenate([h1, h1, h2, h1, h2, h3, h2, h3], 1)


def fresh_of(left, applied):
    a1, a2, a3 = split3(applied)
    right = jnp.concatenate([a1, a2, a1, a3, a2, a1, a3, a2], 0)
    return jnp.dot(left, right, preferred_element_type=F32)


def clear_pads(ref, columns):
    for column in range(columns):
        for slot in list(range(PAD)) + list(range(SLOTS - PAD, SLOTS)):
            ref[column * SLOTS + slot] = jnp.zeros(ref.shape[1:], ref.dtype)


def turn_in(turned_ref, at, rows):
    depth = rows.shape[0]
    padded = jnp.concatenate([rows, jnp.zeros((DEPTH - depth, rows.shape[1]), F32)], 0)
    turned_ref[at] = jnp.transpose(padded).astype(BF16)
    return padded.astype(BF16)


def own_shift(listed_ref):
    middle = COLW + COLW // 2 - 1
    return -jnp.clip(listed_ref[middle, 0] - listed_ref[middle, 3] + COLW, -1, 1)


def halo_shifts(listed_ref):
    middle = COLW // 2 - 1
    before = listed_ref[middle, 0] - listed_ref[middle, 3] + COLW
    after = listed_ref[COLW + middle, 8] - listed_ref[COLW + middle, 5] - COLW
    return jnp.clip(before, -1, 1), jnp.clip(after, -1, 1)


def own_apply(blocks, iter_ref, acc_ref, home, other, across):
    left, right = iter_ref[home], iter_ref[other]
    total = times(left, blocks[0]) + times(iter_ref[home + 1], blocks[1])
    for k in range(3):
        total = total + times(iter_ref[across + k], blocks[2 + k])
    acc_ref[home] += total
    acc_ref[home + 1] += times_turned(left, blocks[1])
    for k in range(3):
        acc_ref[across + k] += times_turned(left, blocks[2 + k])
    acc_ref[other] += times(right, blocks[5]) + times(iter_ref[other + 1], blocks[6])
    acc_ref[other + 1] += times_turned(right, blocks[6])


def sides(listed_ref):
    own_id = listed_ref[COLW + COLW // 2 - 1, 4]
    core = lax.rem(lax.div(own_id, 2 * COLW), 2)
    return core, 1 - core


def pack_kernel(wet_ref, listed_ref, members_ref, initial_ref, off_ref, on_ref):
    count = members_ref.shape[1]
    lane = lax.broadcasted_iota(jnp.int32, members_ref.shape[1:], 1)

    @pl.loop(0, COLW, unroll=2)
    def _(tile):
        for column, ref in zip(sides(listed_ref), (off_ref, on_ref)):
            at = column * COLW + tile
            rows = jnp.where(lane < wet_ref[at], members_ref[at].astype(F32), 0.0)
            ref[tile, :count, :] = rows.astype(BF16)
            ref[tile, count:, :] = initial_ref[at]


def own_kernel(
    listed_hbm, off_ref, on_ref,
    table_ref, padded_ref, block_ref, part_ref,
    wide_ref, turned_ref, iter_ref, listed_ref, sem,
):
    fetch = pltpu.make_async_copy(listed_hbm, listed_ref, sem)
    fetch.start()
    count = off_ref.shape[1] - iter_ref.shape[1]
    make_tapers(table_ref, wide_ref, float(count))
    clear_pads(turned_ref, 2)
    clear_pads(iter_ref, 2)
    part_ref[...] = jnp.zeros_like(part_ref)

    fetch.wait()

    @pl.loop(0, COLW, unroll=4)
    def _(tile):
        for column, ref in zip(sides(listed_ref), (off_ref, on_ref)):
            at = column * SLOTS + PAD + tile
            padded_ref[column * COLW + tile] = turn_in(turned_ref, at, ref[tile, :count, :].astype(F32))
            iter_ref[at] = ref[tile, count:, :]

    moved = own_shift(listed_ref)
    same, next_up = table_ref.at[4], table_ref.at[5]

    @pl.loop(0, COLW, unroll=2)
    def _(r):
        home = PAD + r
        other = SLOTS + PAD + r
        across = other + moved - 1
        blocks = block_ref.at[r]
        left = padded_ref[r]
        make_blocks(turned_ref, home, left, (same, next_up), blocks, 0)
        make_blocks(turned_ref, across, left, [table_ref.at[6 + k] for k in range(3)], blocks, 2)
        make_blocks(turned_ref, other, padded_ref[COLW + r], (same, next_up), blocks, 5)
        own_apply(blocks, iter_ref, part_ref, home, other, across)


def halo_kernel(
    listed_hbm, padded_ref, table_ref, part_ref, off_in_ref, on_in_ref,
    block_ref, off_out_ref, on_out_ref, gram_out_ref,
    turned_ref, iter_ref, last_ref, gram_ref, listed_ref, sem,
):
    fetch = pltpu.make_async_copy(listed_hbm, listed_ref, sem)
    fetch.start()
    rank = iter_ref.shape[1]
    count = off_in_ref.shape[1] - rank
    clear_pads(turned_ref, 2)
    clear_pads(iter_ref, 2)
    gram_ref[...] = jnp.zeros_like(gram_ref)
    last_ref[...] = jnp.zeros_like(last_ref)

    @pl.loop(0, COLW, unroll=4)
    def _(tile):
        for n, ref in enumerate((off_in_ref, on_in_ref)):
            at = n * SLOTS + PAD + tile
            turn_in(turned_ref, at, ref[tile, :count, :].astype(F32))
            iter_ref[at] = ref[tile, count:, :]

    fetch.wait()
    shifts = halo_shifts(listed_ref)
    columns = sides(listed_ref)

    @pl.loop(0, COLW, unroll=2)
    def _(r):
        for n, column in enumerate(columns):
            at = n * SLOTS + PAD + r + jnp.where(column == 0, *shifts) - 1
            make_blocks(
                turned_ref, at, padded_ref[column * COLW + r],
                [table_ref.at[6 * column + k] for k in range(3)], block_ref.at[r], column * 3,
            )
        for n, (column, out_ref) in enumerate(zip(columns, (off_out_ref, on_out_ref))):
            at = n * SLOTS + PAD + r + jnp.where(column == 0, *shifts) - 1
            total = part_ref[column * SLOTS + PAD + r]
            for k in range(3):
                total = total + times(iter_ref[at + k], block_ref[r, column * 3 + k])
            out_ref[r] = total
            gram_add(gram_ref, last_ref[n])
            last_ref[n] = total

    for column in range(2):
        gram_add(gram_ref, last_ref[column])
    gram_out_ref[...] = jnp.broadcast_to(gram_packed(gram_ref, rank)[None], gram_out_ref.shape)


def again_kernel(
    total_points,
    listed_hbm, grams_ref, off_ref, on_ref, off_in_ref, on_in_ref, own_ref, halo_ref,
    out_ref, gram_out_ref,
    iter_ref, acc_ref, gram_ref, listed_ref, sem,
):
    fetch = pltpu.make_async_copy(listed_hbm, listed_ref, sem)
    fetch.start()
    rank = off_ref.shape[1]

    clear_pads(iter_ref, 4)
    gram_ref[...] = jnp.zeros_like(gram_ref)
    left = fresh_left(inverse_factor(jnp.sum(grams_ref[...], 0), rank, total_points))

    fetch.wait()
    off, on = sides(listed_ref)
    held = ((off + 1, off_ref), (on + 1, on_ref), (3 * off, off_in_ref), (3 * on, on_in_ref))

    @pl.loop(0, COLW, unroll=4)
    def _(r):
        for column, ref in held:
            iter_ref[column * SLOTS + PAD + r] = fresh_of(left, ref[r]).astype(BF16)

    acc_ref[...] = jnp.zeros_like(acc_ref)
    moved = own_shift(listed_ref)
    shifts = halo_shifts(listed_ref)

    @pl.loop(0, COLW, unroll=2)
    def _(r):
        home = SLOTS + PAD + r
        own_apply(own_ref.at[r], iter_ref, acc_ref, home, home + SLOTS, home + SLOTS + moved - 1)
        for column in range(2):
            at = column * 3 * SLOTS + PAD + r + shifts[column] - 1
            total = times(iter_ref[at], halo_ref[r, column * 3])
            for k in range(1, 3):
                total = total + times(iter_ref[at + k], halo_ref[r, column * 3 + k])
            acc_ref[home + column * SLOTS] += total

    @pl.loop(0, COLW, unroll=8)
    def _(r):
        for column in range(2):
            total = acc_ref[(column + 1) * SLOTS + PAD + r]
            out_ref[column * COLW + r] = total
            gram_add(gram_ref, total)

    gram_out_ref[...] = jnp.broadcast_to(gram_packed(gram_ref, rank)[None], gram_out_ref.shape)


def last_kernel(total_points, grams_ref, applied_ref, out_hbm, out_ref, sem):
    tiles, rank = applied_ref.shape[:2]
    left = fresh_left(inverse_factor(jnp.sum(grams_ref[...], 0), rank, total_points))
    share = tiles // sem.shape[0]
    sends = []
    for part in range(sem.shape[0]):
        rows = pl.ds(part * share, share)
        for tile in range(part * share, (part + 1) * share):
            out_ref[tile] = fresh_of(left, applied_ref[tile])
        sends.append(pltpu.make_async_copy(out_ref.at[rows], out_hbm.at[rows], sem.at[part]))
        sends[-1].start()
    for send in sends:
        send.wait()


def fold_kernel(in_ref, out_ref):
    out_ref[...] = jnp.broadcast_to(jnp.sum(in_ref[...], 0)[None], out_ref.shape)


def cost(flops, moved):
    return pl.CostEstimate(flops=flops, bytes_accessed=moved, transcendentals=0)


SMEM = pl.BlockSpec(memory_space=pltpu.SMEM)
VMEM = pl.BlockSpec(memory_space=pltpu.VMEM)
HBM = pl.BlockSpec(memory_space=pltpu.HBM)
PARAMS = pltpu.CompilerParams(vmem_limit_bytes=VMEM_LIMIT)
SMALL = pltpu.CompilerParams(vmem_limit_bytes=4 * 1024 * 1024)


def swapped(shard, first):
    lows = range(first, lax.axis_size(TILES_REP) - 1, 2)
    pairs = [pair for i in lows for pair in ((i, i + 1), (i + 1, i))]
    return lax.ppermute(shard, TILES_REP, pairs)


def exchanged(shard, axes):
    return lax.all_to_all(shard, axes, split_axis=0, concat_axis=0, tiled=True)


def gathered(copies, *beside):
    line = lax.axis_size(LINE)
    plane, *beside = lax.optimization_barrier((exchanged(copies, PLANE), *beside))
    summed = pl.pallas_call(
        fold_kernel,
        out_shape=jax.ShapeDtypeStruct((line, *copies.shape[1:]), F32),
        in_specs=[VMEM],
        out_specs=VMEM,
        compiler_params=SMALL,
        name="fold",
    )(plane)
    return exchanged(summed, LINE), *beside


def local(members, initial, wet_counts, tile_coords, neighbours):
    tiles, count, points = members.shape
    rank = initial.shape[1]
    assert tiles == 2 * COLW and points == SIDE * SIDE and rank == 32
    shape = jax.ShapeDtypeStruct
    total_points = float(tiles * lax.axis_size(TILES_REP) * points)
    plane = lax.axis_size(PLANE)
    packed = (8, rank * rank // 8)

    members, initial, wet_counts, neighbours = (
        pltpu.with_memory_space_constraint(x, pltpu.HBM) for x in (members, initial, wet_counts, neighbours)
    )
    pair_s = shape((COLW, count + rank, points), BF16)
    off, on = pl.pallas_call(
        pack_kernel,
        out_shape=(pair_s, pair_s),
        in_specs=[SMEM, SMEM, VMEM, VMEM],
        out_specs=(VMEM, VMEM),
        compiler_params=SMALL,
        name="pack",
    )(wet_counts, neighbours, members, initial)
    off_in, on_in = swapped(off, 1), swapped(on, 0)

    table_s, padded_s = shape((9, points, points), F32), shape((tiles, DEPTH, points), BF16)
    own_s, part_s = shape((COLW, 7, points, points), BF16), shape((2 * SLOTS, rank, points), F32)
    halo_s, half_s = shape((COLW, 6, points, points), BF16), shape((COLW, rank, points), F32)
    listed_s = (pltpu.SMEM(neighbours.shape, jnp.int32), pltpu.SemaphoreType.DMA)
    turned_s = pltpu.VMEM((2 * SLOTS, points, DEPTH), BF16)
    table, padded, own_blocks, part = pl.pallas_call(
        own_kernel,
        out_shape=(table_s, padded_s, own_s, part_s),
        in_specs=[HBM, VMEM, VMEM],
        out_specs=(VMEM,) * 4,
        scratch_shapes=[
            pltpu.VMEM((3, SIDE, 64 * SIDE), F32),
            turned_s,
            pltpu.VMEM((2 * SLOTS, rank, points), BF16),
            *listed_s,
        ],
        compiler_params=PARAMS,
        cost_estimate=cost(96 * 2 * points * points * (DEPTH + rank), 40_000_000),
        name="own_blocks",
    )(neighbours, off, on)

    halo_blocks, off, on, copies = pl.pallas_call(
        halo_kernel,
        out_shape=(halo_s, half_s, half_s, shape((plane, *packed), F32)),
        in_specs=[HBM] + [VMEM] * 5,
        out_specs=(VMEM,) * 4,
        scratch_shapes=[
            turned_s,
            pltpu.VMEM((2 * SLOTS, rank, points), BF16),
            pltpu.VMEM((2, rank, points), F32),
            pltpu.VMEM((3 * rank, 3 * rank), F32),
            *listed_s,
        ],
        compiler_params=PARAMS,
        cost_estimate=cost(48 * 2 * points * points * (DEPTH + rank), 20_000_000),
        name="halo_blocks",
    )(neighbours, padded, table, part, off_in, on_in)

    grams, off_in, on_in = gathered(copies, swapped(off, 1), swapped(on, 0))
    applied, copies = pl.pallas_call(
        functools.partial(again_kernel, total_points),
        out_shape=(shape((tiles, rank, points), F32), shape((plane, *packed), F32)),
        in_specs=[HBM] + [VMEM] * 7,
        out_specs=(VMEM, VMEM),
        scratch_shapes=[
            pltpu.VMEM((4 * SLOTS, rank, points), BF16),
            pltpu.VMEM((4 * SLOTS, rank, points), F32),
            pltpu.VMEM((3 * rank, 3 * rank), F32),
            *listed_s,
        ],
        compiler_params=pltpu.CompilerParams(vmem_limit_bytes=24 * 1024 * 1024),
        name="apply_again",
    )(neighbours, grams, off, on, off_in, on_in, own_blocks, halo_blocks)

    return pl.pallas_call(
        functools.partial(last_kernel, total_points),
        out_shape=shape((tiles, rank, points), F32),
        in_specs=[VMEM, VMEM],
        out_specs=HBM,
        scratch_shapes=[pltpu.VMEM((tiles, rank, points), F32), pltpu.SemaphoreType.DMA((4,))],
        compiler_params=SMALL,
        name="last_fresh",
    )(*gathered(copies), applied)


def solution(mesh):
    split = Mesh(mesh.devices.reshape(*SPLIT, mesh.shape["rep"]), TILES_REP)
    return jax.shard_map(
        local,
        mesh=split,
        in_specs=(
            P(TILES_REP, None, None),
            P(TILES_REP, None, None),
            P(TILES_REP),
            P(TILES_REP, None),
            P(TILES_REP, None),
        ),
        out_specs=P(TILES_REP, None, None),
        check_vma=False,
    )
```

```python
import functools

import jax
import jax.numpy as jnp
from jax import lax
from jax.experimental import pallas as pl
from jax.experimental.pallas import tpu as pltpu
from jax.sharding import Mesh
from jax.sharding import PartitionSpec as P

SIDE = 16
COLW = 8
SPLIT = (4, 16, 4)
TILES_REP = ("tiles_0", "tiles_1", "tiles_2", "rep")
PLANE = ("tiles_0", "tiles_2", "rep")
LINE = ("tiles_1",)
PAD = 2
SLOTS = COLW + 2 * PAD
DEPTH = 128
F32 = jnp.float32
BF16 = jnp.bfloat16
VMEM_LIMIT = 20 * 1024 * 1024


def gaspari(scaled):
    clamped = jnp.maximum(scaled, 1.0)
    inner = (((-0.25 * scaled + 0.5) * scaled + 0.625) * scaled - 5.0 / 3.0) * scaled * scaled + 1.0
    outer = (
        ((((scaled / 12.0 - 0.5) * scaled + 0.625) * scaled + 5.0 / 3.0) * scaled - 5.0) * scaled
        + 4.0
        - 2.0 / (3.0 * clamped)
    )
    return jnp.where(scaled <= 1.0, inner, jnp.where(scaled <= 2.0, outer, 0.0))


def make_tapers(table_ref, wide_ref, members):
    shape = (SIDE, 64 * SIDE)
    lane = lax.broadcasted_iota(jnp.int32, shape, 1)
    sub = lax.broadcasted_iota(jnp.int32, shape, 0)
    apart_row = (2 * SIDE - 1 - lane // SIDE).astype(F32)
    for k in range(3):
        apart_col = (SIDE * (k - 1) + sub - lane % SIDE).astype(F32)
        distance = jnp.sqrt(apart_row * apart_row + apart_col * apart_col)
        wide_ref[k] = gaspari(distance / (0.5 * SIDE)) / (members - 1.0)
    per_group = 128 // SIDE
    for k in range(3):
        wide = wide_ref[k]
        for turn in range(per_group):
            rolled = pltpu.roll(wide, 64 * SIDE - turn * SIDE, 1) if turn else wide
            for d in range(3):
                for row in range(SIDE):
                    first = 2 * SIDE - 1 - SIDE * (d - 1) - row
                    if first % per_group == turn and (d, k) != (1, 0):
                        start = (first - turn) * SIDE
                        table_ref[d * 3 + k, row * SIDE : (row + 1) * SIDE, :] = rolled[
                            :, start : start + SIDE * SIDE
                        ]


def split3(x):
    high = x.astype(BF16)
    rest = x - high.astype(F32)
    mid = rest.astype(BF16)
    low = (rest - mid.astype(F32)).astype(BF16)
    return high, mid, low


def make_blocks(turned_ref, at, right, tables, block_ref, first):
    points = right.shape[1]
    count = len(tables)
    for n, table in enumerate(tables):
        product = jnp.dot(turned_ref[at + n], right, preferred_element_type=F32)
        block_ref[first + n] = (product * table[...]).astype(BF16)


def times(rows, block):
    return jnp.dot(rows, block, preferred_element_type=F32)


def times_turned(rows, block):
    return lax.dot_general(rows, block, (((1,), (1,)), ((), ())), preferred_element_type=F32)


def gram_add(gram_ref, applied):
    parts = jnp.concatenate(split3(applied), 0)
    gram_ref[...] += lax.dot_general(parts, parts, (((1,), (1,)), ((), ())), preferred_element_type=F32)


def gram_packed(gram_ref, rank):
    full = gram_ref[...]

    def piece(a, b):
        return full[a * rank : (a + 1) * rank, b * rank : (b + 1) * rank]

    small = piece(0, 2) + piece(2, 0) + piece(1, 1) + (piece(1, 2) + piece(2, 1))
    total = piece(0, 0) + (piece(0, 1) + piece(1, 0) + small)
    return jnp.concatenate([total[8 * q : 8 * q + 8, :] for q in range(rank // 8)], 1)


def inverse_factor(packed, rank, total_points):
    gram = jnp.concatenate([packed[:, rank * q : rank * (q + 1)] for q in range(rank // 8)], 0)
    gram = gram / total_points
    work = jnp.concatenate([gram, jnp.zeros((rank, 128 - rank), F32)], 1)
    lane = lax.broadcasted_iota(jnp.int32, (rank, 128), 1)
    sub = lax.broadcasted_iota(jnp.int32, (rank, 128), 0)
    work = jnp.where(lane == sub + rank, 1.0, work)
    groups = []
    for step in range(0, rank, 4):
        base = step // 8 * 8
        at = step - base
        below = work[base:, :]
        columns = [jnp.broadcast_to(below[:, step + j : step + j + 1], below.shape) for j in range(4)]

        def pivot(i, j):
            return columns[j][at + i : at + i + 1, :]

        r0, r1, r2, r3 = (below[at + i : at + i + 1, :] for i in range(4))
        a00, a10, a11 = pivot(0, 0), pivot(1, 0), pivot(1, 1)
        over = 1.0 / (a00 * a11 - a10 * a10)
        i00, i10, i11 = a11 * over, -a10 * over, a00 * over
        b00, b01, b10, b11 = pivot(2, 0), pivot(2, 1), pivot(3, 0), pivot(3, 1)
        y00, y01 = b00 * i00 + b01 * i10, b00 * i10 + b01 * i11
        y10, y11 = b10 * i00 + b11 * i10, b10 * i10 + b11 * i11
        s00 = pivot(2, 2) - (y00 * b00 + y01 * b01)
        s10 = pivot(3, 2) - (y10 * b00 + y11 * b01)
        s11 = pivot(3, 3) - (y10 * b10 + y11 * b11)
        w2 = r2 - (y00 * r0 + y01 * r1)
        w3 = r3 - (y10 * r0 + y11 * r1)
        q1, q3 = a10 / a00, s10 / s00
        done = (
            r0 / jnp.sqrt(a00),
            (r1 - q1 * r0) / jnp.sqrt(a11 - q1 * a10),
            w2 / jnp.sqrt(s00),
            (w3 - q3 * w2) / jnp.sqrt(s11 - q3 * s10),
        )
        if at == 0:
            groups.append(jnp.zeros((8, 128), F32))
        for i in range(4):
            groups[-1] = jnp.where(sub[:8, :] == at + i, done[i], groups[-1])
        if step + 4 < rank:
            over = 1.0 / (s00 * s11 - s10 * s10)
            z2 = (s11 * w2 - s10 * w3) * over
            z3 = (s00 * w3 - s10 * w2) * over
            z0 = i00 * r0 + i10 * r1 - (y00 * z2 + y10 * z3)
            z1 = i10 * r0 + i11 * r1 - (y01 * z2 + y11 * z3)
            left = below - (columns[0] * z0 + columns[1] * z1) - (columns[2] * z2 + columns[3] * z3)
            if at == 0:
                left = jnp.where(sub[base:, :] > step + 3, left, below)
            work = jnp.concatenate([work[:base, :], left], 0) if base else left
    return jnp.concatenate(groups, 0)[:, rank : 2 * rank]


def fresh_left(inverse):
    h1, h2, h3 = split3(inverse)
    return jnp.concatenate([h1, h1, h2, h1, h2, h3, h2, h3], 1)


def fresh_of(left, applied):
    a1, a2, a3 = split3(applied)
    right = jnp.concatenate([a1, a2, a1, a3, a2, a1, a3, a2], 0)
    return jnp.dot(left, right, preferred_element_type=F32)


def clear_pads(ref, columns):
    for column in range(columns):
        for slot in list(range(PAD)) + list(range(SLOTS - PAD, SLOTS)):
            ref[column * SLOTS + slot] = jnp.zeros(ref.shape[1:], ref.dtype)


def turn_in(turned_ref, at, rows):
    depth = rows.shape[0]
    padded = jnp.concatenate([rows, jnp.zeros((DEPTH - depth, rows.shape[1]), F32)], 0)
    turned_ref[at] = jnp.transpose(padded).astype(BF16)
    return padded.astype(BF16)


def own_shift(listed_ref):
    middle = COLW + COLW // 2 - 1
    return -jnp.clip(listed_ref[middle, 0] - listed_ref[middle, 3] + COLW, -1, 1)


def halo_shifts(listed_ref):
    middle = COLW // 2 - 1
    before = listed_ref[middle, 0] - listed_ref[middle, 3] + COLW
    after = listed_ref[COLW + middle, 8] - listed_ref[COLW + middle, 5] - COLW
    return jnp.clip(before, -1, 1), jnp.clip(after, -1, 1)


def own_apply(blocks, iter_ref, acc_ref, home, other, across):
    left, right = iter_ref[home], iter_ref[other]
    total = times(left, blocks[0]) + times(iter_ref[home + 1], blocks[1])
    for k in range(3):
        total = total + times(iter_ref[across + k], blocks[2 + k])
    acc_ref[home] += total
    acc_ref[home + 1] += times_turned(left, blocks[1])
    for k in range(3):
        acc_ref[across + k] += times_turned(left, blocks[2 + k])
    acc_ref[other] += times(right, blocks[5]) + times(iter_ref[other + 1], blocks[6])
    acc_ref[other + 1] += times_turned(right, blocks[6])


def sides(listed_ref):
    own_id = listed_ref[COLW + COLW // 2 - 1, 4]
    core = lax.rem(lax.div(own_id, 2 * COLW), 2)
    return core, 1 - core


def pack_kernel(wet_ref, listed_ref, members_ref, initial_ref, off_ref, on_ref):
    count = members_ref.shape[1]
    lane = lax.broadcasted_iota(jnp.int32, members_ref.shape[1:], 1)

    @pl.loop(0, COLW, unroll=2)
    def _(tile):
        for column, ref in zip(sides(listed_ref), (off_ref, on_ref)):
            at = column * COLW + tile
            rows = jnp.where(lane < wet_ref[at], members_ref[at].astype(F32), 0.0)
            ref[tile, :count, :] = rows.astype(BF16)
            ref[tile, count:, :] = initial_ref[at]


def own_kernel(
    listed_hbm, off_ref, on_ref,
    table_ref, padded_ref, block_ref, part_ref,
    wide_ref, turned_ref, iter_ref, listed_ref, sem,
):
    fetch = pltpu.make_async_copy(listed_hbm, listed_ref, sem)
    fetch.start()
    count = off_ref.shape[1] - iter_ref.shape[1]
    make_tapers(table_ref, wide_ref, float(count))
    clear_pads(turned_ref, 2)
    clear_pads(iter_ref, 2)
    part_ref[...] = jnp.zeros_like(part_ref)

    fetch.wait()

    @pl.loop(0, COLW, unroll=4)
    def _(tile):
        for column, ref in zip(sides(listed_ref), (off_ref, on_ref)):
            at = column * SLOTS + PAD + tile
            padded_ref[column * COLW + tile] = turn_in(turned_ref, at, ref[tile, :count, :].astype(F32))
            iter_ref[at] = ref[tile, count:, :]

    moved = own_shift(listed_ref)
    same, next_up = table_ref.at[4], table_ref.at[5]

    @pl.loop(0, COLW, unroll=4)
    def _(r):
        home = PAD + r
        other = SLOTS + PAD + r
        across = other + moved - 1
        blocks = block_ref.at[r]
        left = padded_ref[r]
        make_blocks(turned_ref, home, left, (same, next_up), blocks, 0)
        make_blocks(turned_ref, across, left, [table_ref.at[6 + k] for k in range(3)], blocks, 2)
        make_blocks(turned_ref, other, padded_ref[COLW + r], (same, next_up), blocks, 5)
        own_apply(blocks, iter_ref, part_ref, home, other, across)


def halo_kernel(
    listed_hbm, padded_ref, table_ref, part_ref, off_in_ref, on_in_ref,
    block_ref, off_out_ref, on_out_ref, gram_out_ref,
    turned_ref, iter_ref, last_ref, gram_ref, listed_ref, sem,
):
    fetch = pltpu.make_async_copy(listed_hbm, listed_ref, sem)
    fetch.start()
    rank = iter_ref.shape[1]
    count = off_in_ref.shape[1] - rank
    clear_pads(turned_ref, 2)
    clear_pads(iter_ref, 2)
    gram_ref[...] = jnp.zeros_like(gram_ref)
    last_ref[...] = jnp.zeros_like(last_ref)

    @pl.loop(0, COLW, unroll=4)
    def _(tile):
        for n, ref in enumerate((off_in_ref, on_in_ref)):
            at = n * SLOTS + PAD + tile
            turn_in(turned_ref, at, ref[tile, :count, :].astype(F32))
            iter_ref[at] = ref[tile, count:, :]

    fetch.wait()
    shifts = halo_shifts(listed_ref)
    columns = sides(listed_ref)

    @pl.loop(0, COLW, unroll=4)
    def _(r):
        for n, column in enumerate(columns):
            at = n * SLOTS + PAD + r + jnp.where(column == 0, *shifts) - 1
            make_blocks(
                turned_ref, at, padded_ref[column * COLW + r],
                [table_ref.at[6 * column + k] for k in range(3)], block_ref.at[r], n * 3,
            )
        for n, (column, out_ref) in enumerate(zip(columns, (off_out_ref, on_out_ref))):
            at = n * SLOTS + PAD + r + jnp.where(column == 0, *shifts) - 1
            total = part_ref[column * SLOTS + PAD + r]
            for k in range(3):
                total = total + times(iter_ref[at + k], block_ref[r, n * 3 + k])
            out_ref[r] = total
            gram_add(gram_ref, last_ref[n])
            last_ref[n] = total

    for column in range(2):
        gram_add(gram_ref, last_ref[column])
    gram_out_ref[...] = jnp.broadcast_to(gram_packed(gram_ref, rank)[None], gram_out_ref.shape)


def again_kernel(
    total_points,
    listed_hbm, grams_ref, off_ref, on_ref, off_in_ref, on_in_ref, own_ref, halo_ref,
    out_ref, gram_out_ref,
    iter_ref, acc_ref, gram_ref, listed_ref, sem,
):
    fetch = pltpu.make_async_copy(listed_hbm, listed_ref, sem)
    fetch.start()
    rank = off_ref.shape[1]

    clear_pads(iter_ref, 4)
    gram_ref[...] = jnp.zeros_like(gram_ref)
    left = fresh_left(inverse_factor(jnp.sum(grams_ref[...], 0), rank, total_points))

    fetch.wait()
    off, on = sides(listed_ref)
    held = ((off + 1, off_ref), (on + 1, on_ref), (3 * off, off_in_ref), (3 * on, on_in_ref))

    @pl.loop(0, COLW, unroll=4)
    def _(r):
        for column, ref in held:
            iter_ref[column * SLOTS + PAD + r] = fresh_of(left, ref[r]).astype(BF16)

    acc_ref[...] = jnp.zeros_like(acc_ref)
    moved = own_shift(listed_ref)
    shifts = halo_shifts(listed_ref)

    @pl.loop(0, COLW, unroll=4)
    def _(r):
        home = SLOTS + PAD + r
        own_apply(own_ref.at[r], iter_ref, acc_ref, home, home + SLOTS, home + SLOTS + moved - 1)
        for n, column in enumerate((off, on)):
            at = column * 3 * SLOTS + PAD + r + jnp.where(column == 0, *shifts) - 1
            total = times(iter_ref[at], halo_ref[r, n * 3])
            for k in range(1, 3):
                total = total + times(iter_ref[at + k], halo_ref[r, n * 3 + k])
            acc_ref[home + column * SLOTS] += total

    @pl.loop(0, COLW, unroll=8)
    def _(r):
        for column in range(2):
            total = acc_ref[(column + 1) * SLOTS + PAD + r]
            out_ref[column * COLW + r] = total
            gram_add(gram_ref, total)

    gram_out_ref[...] = jnp.broadcast_to(gram_packed(gram_ref, rank)[None], gram_out_ref.shape)


def last_kernel(total_points, grams_ref, applied_ref, out_hbm, out_ref, sem):
    tiles, rank = applied_ref.shape[:2]
    left = fresh_left(inverse_factor(jnp.sum(grams_ref[...], 0), rank, total_points))
    share = tiles // sem.shape[0]
    sends = []
    for part in range(sem.shape[0]):
        rows = pl.ds(part * share, share)
        for tile in range(part * share, (part + 1) * share):
            out_ref[tile] = fresh_of(left, applied_ref[tile])
        sends.append(pltpu.make_async_copy(out_ref.at[rows], out_hbm.at[rows], sem.at[part]))
        sends[-1].start()
    for send in sends:
        send.wait()


def fold_kernel(in_ref, out_ref):
    out_ref[...] = jnp.broadcast_to(jnp.sum(in_ref[...], 0)[None], out_ref.shape)


def cost(flops, moved):
    return pl.CostEstimate(flops=flops, bytes_accessed=moved, transcendentals=0)


SMEM = pl.BlockSpec(memory_space=pltpu.SMEM)
VMEM = pl.BlockSpec(memory_space=pltpu.VMEM)
HBM = pl.BlockSpec(memory_space=pltpu.HBM)
PARAMS = pltpu.CompilerParams(vmem_limit_bytes=VMEM_LIMIT)
SMALL = pltpu.CompilerParams(vmem_limit_bytes=4 * 1024 * 1024)


def swapped(shard, first):
    lows = range(first, lax.axis_size(TILES_REP) - 1, 2)
    pairs = [pair for i in lows for pair in ((i, i + 1), (i + 1, i))]
    return lax.ppermute(shard, TILES_REP, pairs)


def exchanged(shard, axes):
    return lax.all_to_all(shard, axes, split_axis=0, concat_axis=0, tiled=True)


def gathered(copies, *beside):
    line = lax.axis_size(LINE)
    plane, *beside = lax.optimization_barrier((exchanged(copies, PLANE), *beside))
    summed = pl.pallas_call(
        fold_kernel,
        out_shape=jax.ShapeDtypeStruct((line, *copies.shape[1:]), F32),
        in_specs=[VMEM],
        out_specs=VMEM,
        compiler_params=SMALL,
        name="fold",
    )(plane)
    return exchanged(summed, LINE), *beside


def local(members, initial, wet_counts, tile_coords, neighbours):
    tiles, count, points = members.shape
    rank = initial.shape[1]
    assert tiles == 2 * COLW and points == SIDE * SIDE and rank == 32
    shape = jax.ShapeDtypeStruct
    total_points = float(tiles * lax.axis_size(TILES_REP) * points)
    plane = lax.axis_size(PLANE)
    packed = (8, rank * rank // 8)

    members, initial, wet_counts, neighbours = (
        pltpu.with_memory_space_constraint(x, pltpu.HBM) for x in (members, initial, wet_counts, neighbours)
    )
    pair_s = shape((COLW, count + rank, points), BF16)
    off, on = pl.pallas_call(
        pack_kernel,
        out_shape=(pair_s, pair_s),
        in_specs=[SMEM, SMEM, VMEM, VMEM],
        out_specs=(VMEM, VMEM),
        compiler_params=SMALL,
        name="pack",
    )(wet_counts, neighbours, members, initial)
    off_in, on_in = swapped(off, 1), swapped(on, 0)

    table_s, padded_s = shape((9, points, points), F32), shape((tiles, DEPTH, points), BF16)
    own_s, part_s = shape((COLW, 7, points, points), BF16), shape((2 * SLOTS, rank, points), F32)
    halo_s, half_s = shape((COLW, 6, points, points), BF16), shape((COLW, rank, points), F32)
    listed_s = (pltpu.SMEM(neighbours.shape, jnp.int32), pltpu.SemaphoreType.DMA)
    turned_s = pltpu.VMEM((2 * SLOTS, points, DEPTH), BF16)
    table, padded, own_blocks, part = pl.pallas_call(
        own_kernel,
        out_shape=(table_s, padded_s, own_s, part_s),
        in_specs=[HBM, VMEM, VMEM],
        out_specs=(VMEM,) * 4,
        scratch_shapes=[
            pltpu.VMEM((3, SIDE, 64 * SIDE), F32),
            turned_s,
            pltpu.VMEM((2 * SLOTS, rank, points), BF16),
            *listed_s,
        ],
        compiler_params=PARAMS,
        cost_estimate=cost(96 * 2 * points * points * (DEPTH + rank), 40_000_000),
        name="own_blocks",
    )(neighbours, off, on)

    halo_blocks, off, on, copies = pl.pallas_call(
        halo_kernel,
        out_shape=(halo_s, half_s, half_s, shape((plane, *packed), F32)),
        in_specs=[HBM] + [VMEM] * 5,
        out_specs=(VMEM,) * 4,
        scratch_shapes=[
            turned_s,
            pltpu.VMEM((2 * SLOTS, rank, points), BF16),
            pltpu.VMEM((2, rank, points), F32),
            pltpu.VMEM((3 * rank, 3 * rank), F32),
            *listed_s,
        ],
        compiler_params=PARAMS,
        cost_estimate=cost(48 * 2 * points * points * (DEPTH + rank), 20_000_000),
        name="halo_blocks",
    )(neighbours, padded, table, part, off_in, on_in)

    grams, off_in, on_in = gathered(copies, swapped(off, 1), swapped(on, 0))
    applied, copies = pl.pallas_call(
        functools.partial(again_kernel, total_points),
        out_shape=(shape((tiles, rank, points), F32), shape((plane, *packed), F32)),
        in_specs=[HBM] + [VMEM] * 7,
        out_specs=(VMEM, VMEM),
        scratch_shapes=[
            pltpu.VMEM((4 * SLOTS, rank, points), BF16),
            pltpu.VMEM((4 * SLOTS, rank, points), F32),
            pltpu.VMEM((3 * rank, 3 * rank), F32),
            *listed_s,
        ],
        compiler_params=pltpu.CompilerParams(vmem_limit_bytes=24 * 1024 * 1024),
        name="apply_again",
    )(neighbours, grams, off, on, off_in, on_in, own_blocks, halo_blocks)

    return pl.pallas_call(
        functools.partial(last_kernel, total_points),
        out_shape=shape((tiles, rank, points), F32),
        in_specs=[VMEM, VMEM],
        out_specs=HBM,
        scratch_shapes=[pltpu.VMEM((tiles, rank, points), F32), pltpu.SemaphoreType.DMA((4,))],
        compiler_params=SMALL,
        name="last_fresh",
    )(*gathered(copies), applied)


def solution(mesh):
    split = Mesh(mesh.devices.reshape(*SPLIT, mesh.shape["rep"]), TILES_REP)
    return jax.shard_map(
        local,
        mesh=split,
        in_specs=(
            P(TILES_REP, None, None),
            P(TILES_REP, None, None),
            P(TILES_REP),
            P(TILES_REP, None),
            P(TILES_REP, None),
        ),
        out_specs=P(TILES_REP, None, None),
        check_vma=False,
    )
```

```python
import functools

import jax
import jax.numpy as jnp
from jax import lax
from jax.experimental import pallas as pl
from jax.experimental.pallas import tpu as pltpu
from jax.sharding import Mesh
from jax.sharding import PartitionSpec as P

SIDE = 16
COLW = 8
SPLIT = (4, 16, 4)
TILES_REP = ("tiles_0", "tiles_1", "tiles_2", "rep")
PLANE = ("tiles_0", "tiles_2", "rep")
LINE = ("tiles_1",)
PAD = 2
SLOTS = COLW + 2 * PAD
DEPTH = 128
F32 = jnp.float32
BF16 = jnp.bfloat16
VMEM_LIMIT = 20 * 1024 * 1024


def gaspari(scaled):
    clamped = jnp.maximum(scaled, 1.0)
    inner = (((-0.25 * scaled + 0.5) * scaled + 0.625) * scaled - 5.0 / 3.0) * scaled * scaled + 1.0
    outer = (
        ((((scaled / 12.0 - 0.5) * scaled + 0.625) * scaled + 5.0 / 3.0) * scaled - 5.0) * scaled
        + 4.0
        - 2.0 / (3.0 * clamped)
    )
    return jnp.where(scaled <= 1.0, inner, jnp.where(scaled <= 2.0, outer, 0.0))


def make_tapers(table_ref, wide_ref, members):
    shape = (SIDE, 64 * SIDE)
    lane = lax.broadcasted_iota(jnp.int32, shape, 1)
    sub = lax.broadcasted_iota(jnp.int32, shape, 0)
    apart_row = (2 * SIDE - 1 - lane // SIDE).astype(F32)
    for k in range(3):
        apart_col = (SIDE * (k - 1) + sub - lane % SIDE).astype(F32)
        distance = jnp.sqrt(apart_row * apart_row + apart_col * apart_col)
        wide_ref[k] = gaspari(distance / (0.5 * SIDE)) / (members - 1.0)
    per_group = 128 // SIDE
    for k in range(3):
        wide = wide_ref[k]
        for turn in range(per_group):
            rolled = pltpu.roll(wide, 64 * SIDE - turn * SIDE, 1) if turn else wide
            for d in range(3):
                for row in range(SIDE):
                    first = 2 * SIDE - 1 - SIDE * (d - 1) - row
                    if first % per_group == turn and (d, k) != (1, 0):
                        start = (first - turn) * SIDE
                        table_ref[d * 3 + k, row * SIDE : (row + 1) * SIDE, :] = rolled[
                            :, start : start + SIDE * SIDE
                        ]


def split3(x):
    high = x.astype(BF16)
    rest = x - high.astype(F32)
    mid = rest.astype(BF16)
    low = (rest - mid.astype(F32)).astype(BF16)
    return high, mid, low


def make_blocks(turned_ref, at, right, tables, block_ref, first):
    points = right.shape[1]
    count = len(tables)
    for n, table in enumerate(tables):
        product = jnp.dot(turned_ref[at + n], right, preferred_element_type=F32)
        block_ref[first + n] = (product * table[...]).astype(BF16)


def times(rows, block):
    return jnp.dot(rows, block, preferred_element_type=F32)


def times_turned(rows, block):
    return lax.dot_general(rows, block, (((1,), (1,)), ((), ())), preferred_element_type=F32)


def gram_add(gram_ref, applied):
    parts = jnp.concatenate(split3(applied), 0)
    gram_ref[...] += lax.dot_general(parts, parts, (((1,), (1,)), ((), ())), preferred_element_type=F32)


def gram_packed(gram_ref, rank):
    full = gram_ref[...]

    def piece(a, b):
        return full[a * rank : (a + 1) * rank, b * rank : (b + 1) * rank]

    small = piece(0, 2) + piece(2, 0) + piece(1, 1) + (piece(1, 2) + piece(2, 1))
    total = piece(0, 0) + (piece(0, 1) + piece(1, 0) + small)
    return jnp.concatenate([total[8 * q : 8 * q + 8, :] for q in range(rank // 8)], 1)


def inverse_factor(packed, rank, total_points):
    gram = jnp.concatenate([packed[:, rank * q : rank * (q + 1)] for q in range(rank // 8)], 0)
    gram = gram / total_points
    work = jnp.concatenate([gram, jnp.zeros((rank, 128 - rank), F32)], 1)
    lane = lax.broadcasted_iota(jnp.int32, (rank, 128), 1)
    sub = lax.broadcasted_iota(jnp.int32, (rank, 128), 0)
    work = jnp.where(lane == sub + rank, 1.0, work)
    groups = []
    for step in range(0, rank, 4):
        base = step // 8 * 8
        at = step - base
        below = work[base:, :]
        columns = [jnp.broadcast_to(below[:, step + j : step + j + 1], below.shape) for j in range(4)]

        def pivot(i, j):
            return columns[j][at + i : at + i + 1, :]

        r0, r1, r2, r3 = (below[at + i : at + i + 1, :] for i in range(4))
        a00, a10, a11 = pivot(0, 0), pivot(1, 0), pivot(1, 1)
        over = 1.0 / (a00 * a11 - a10 * a10)
        i00, i10, i11 = a11 * over, -a10 * over, a00 * over
        b00, b01, b10, b11 = pivot(2, 0), pivot(2, 1), pivot(3, 0), pivot(3, 1)
        y00, y01 = b00 * i00 + b01 * i10, b00 * i10 + b01 * i11
        y10, y11 = b10 * i00 + b11 * i10, b10 * i10 + b11 * i11
        s00 = pivot(2, 2) - (y00 * b00 + y01 * b01)
        s10 = pivot(3, 2) - (y10 * b00 + y11 * b01)
        s11 = pivot(3, 3) - (y10 * b10 + y11 * b11)
        w2 = r2 - (y00 * r0 + y01 * r1)
        w3 = r3 - (y10 * r0 + y11 * r1)
        q1, q3 = a10 / a00, s10 / s00
        done = (
            r0 / jnp.sqrt(a00),
            (r1 - q1 * r0) / jnp.sqrt(a11 - q1 * a10),
            w2 / jnp.sqrt(s00),
            (w3 - q3 * w2) / jnp.sqrt(s11 - q3 * s10),
        )
        if at == 0:
            groups.append(jnp.zeros((8, 128), F32))
        for i in range(4):
            groups[-1] = jnp.where(sub[:8, :] == at + i, done[i], groups[-1])
        if step + 4 < rank:
            over = 1.0 / (s00 * s11 - s10 * s10)
            z2 = (s11 * w2 - s10 * w3) * over
            z3 = (s00 * w3 - s10 * w2) * over
            z0 = i00 * r0 + i10 * r1 - (y00 * z2 + y10 * z3)
            z1 = i10 * r0 + i11 * r1 - (y01 * z2 + y11 * z3)
            left = below - (columns[0] * z0 + columns[1] * z1) - (columns[2] * z2 + columns[3] * z3)
            if at == 0:
                left = jnp.where(sub[base:, :] > step + 3, left, below)
            work = jnp.concatenate([work[:base, :], left], 0) if base else left
    return jnp.concatenate(groups, 0)[:, rank : 2 * rank]


def fresh_left(inverse):
    h1, h2, h3 = split3(inverse)
    return jnp.concatenate([h1, h1, h2, h1, h2, h3, h2, h3], 1)


def fresh_of(left, applied):
    a1, a2, a3 = split3(applied)
    right = jnp.concatenate([a1, a2, a1, a3, a2, a1, a3, a2], 0)
    return jnp.dot(left, right, preferred_element_type=F32)


def clear_pads(ref, columns):
    for column in range(columns):
        for slot in list(range(PAD)) + list(range(SLOTS - PAD, SLOTS)):
            ref[column * SLOTS + slot] = jnp.zeros(ref.shape[1:], ref.dtype)


def turn_in(turned_ref, at, rows):
    depth = rows.shape[0]
    padded = jnp.concatenate([rows, jnp.zeros((DEPTH - depth, rows.shape[1]), F32)], 0)
    turned_ref[at] = jnp.transpose(padded).astype(BF16)
    return padded.astype(BF16)


def own_shift(listed_ref):
    middle = COLW + COLW // 2 - 1
    return -jnp.clip(listed_ref[middle, 0] - listed_ref[middle, 3] + COLW, -1, 1)


def halo_shifts(listed_ref):
    middle = COLW // 2 - 1
    before = listed_ref[middle, 0] - listed_ref[middle, 3] + COLW
    after = listed_ref[COLW + middle, 8] - listed_ref[COLW + middle, 5] - COLW
    return jnp.clip(before, -1, 1), jnp.clip(after, -1, 1)


def own_apply(blocks, iter_ref, acc_ref, home, other, across):
    left, right = iter_ref[home], iter_ref[other]
    total = times(left, blocks[0]) + times(iter_ref[home + 1], blocks[1])
    for k in range(3):
        total = total + times(iter_ref[across + k], blocks[2 + k])
    acc_ref[home] += total
    acc_ref[home + 1] += times_turned(left, blocks[1])
    for k in range(3):
        acc_ref[across + k] += times_turned(left, blocks[2 + k])
    acc_ref[other] += times(right, blocks[5]) + times(iter_ref[other + 1], blocks[6])
    acc_ref[other + 1] += times_turned(right, blocks[6])


def sides(listed_ref):
    own_id = listed_ref[COLW + COLW // 2 - 1, 4]
    core = lax.rem(lax.div(own_id, 2 * COLW), 2)
    return core, 1 - core


def pack_kernel(wet_ref, listed_ref, members_ref, initial_ref, off_ref, on_ref):
    count = members_ref.shape[1]
    lane = lax.broadcasted_iota(jnp.int32, members_ref.shape[1:], 1)

    @pl.loop(0, COLW, unroll=2)
    def _(tile):
        for column, ref in zip(sides(listed_ref), (off_ref, on_ref)):
            at = column * COLW + tile
            rows = jnp.where(lane < wet_ref[at], members_ref[at].astype(F32), 0.0)
            ref[tile, :count, :] = rows.astype(BF16)
            ref[tile, count:, :] = initial_ref[at]


def own_kernel(
    listed_hbm, off_ref, on_ref,
    table_ref, padded_ref, block_ref, part_ref,
    wide_ref, turned_ref, iter_ref, listed_ref, sem,
):
    fetch = pltpu.make_async_copy(listed_hbm, listed_ref, sem)
    fetch.start()
    count = off_ref.shape[1] - iter_ref.shape[1]
    make_tapers(table_ref, wide_ref, float(count))
    clear_pads(turned_ref, 2)
    clear_pads(iter_ref, 2)
    part_ref[...] = jnp.zeros_like(part_ref)

    fetch.wait()

    @pl.loop(0, COLW, unroll=4)
    def _(tile):
        for column, ref in zip(sides(listed_ref), (off_ref, on_ref)):
            at = column * SLOTS + PAD + tile
            padded_ref[column * COLW + tile] = turn_in(turned_ref, at, ref[tile, :count, :].astype(F32))
            iter_ref[at] = ref[tile, count:, :]

    moved = own_shift(listed_ref)
    same, next_up = table_ref.at[4], table_ref.at[5]

    @pl.loop(0, COLW, unroll=4)
    def _(r):
        home = PAD + r
        other = SLOTS + PAD + r
        across = other + moved - 1
        blocks = block_ref.at[r]
        left = padded_ref[r]
        make_blocks(turned_ref, home, left, (same, next_up), blocks, 0)
        make_blocks(turned_ref, across, left, [table_ref.at[6 + k] for k in range(3)], blocks, 2)
        make_blocks(turned_ref, other, padded_ref[COLW + r], (same, next_up), blocks, 5)
        own_apply(blocks, iter_ref, part_ref, home, other, across)


def halo_kernel(
    listed_hbm, padded_ref, table_ref, part_ref, off_in_ref, on_in_ref,
    block_ref, off_out_ref, on_out_ref, gram_out_ref,
    turned_ref, iter_ref, last_ref, gram_ref, listed_ref, sem,
):
    fetch = pltpu.make_async_copy(listed_hbm, listed_ref, sem)
    fetch.start()
    rank = iter_ref.shape[1]
    count = off_in_ref.shape[1] - rank
    clear_pads(turned_ref, 2)
    clear_pads(iter_ref, 2)
    gram_ref[...] = jnp.zeros_like(gram_ref)
    last_ref[...] = jnp.zeros_like(last_ref)

    @pl.loop(0, COLW, unroll=4)
    def _(tile):
        for n, ref in enumerate((off_in_ref, on_in_ref)):
            at = n * SLOTS + PAD + tile
            turn_in(turned_ref, at, ref[tile, :count, :].astype(F32))
            iter_ref[at] = ref[tile, count:, :]

    fetch.wait()
    shifts = halo_shifts(listed_ref)
    columns = sides(listed_ref)

    @pl.loop(0, COLW, unroll=4)
    def _(r):
        for n, column in enumerate(columns):
            at = n * SLOTS + PAD + r + jnp.where(column == 0, *shifts) - 1
            make_blocks(
                turned_ref, at, padded_ref[column * COLW + r],
                [table_ref.at[6 * column + k] for k in range(3)], block_ref.at[r], n * 3,
            )
        for n, (column, out_ref) in enumerate(zip(columns, (off_out_ref, on_out_ref))):
            at = n * SLOTS + PAD + r + jnp.where(column == 0, *shifts) - 1
            total = part_ref[column * SLOTS + PAD + r]
            for k in range(3):
                total = total + times(iter_ref[at + k], block_ref[r, n * 3 + k])
            out_ref[r] = total
            gram_add(gram_ref, last_ref[n])
            last_ref[n] = total

    for column in range(2):
        gram_add(gram_ref, last_ref[column])
    gram_out_ref[...] = jnp.broadcast_to(gram_packed(gram_ref, rank)[None], gram_out_ref.shape)


def again_kernel(
    total_points,
    listed_hbm, grams_ref, off_ref, on_ref, off_in_ref, on_in_ref, own_ref, halo_ref,
    out_ref, gram_out_ref,
    iter_ref, acc_ref, gram_ref, listed_ref, sem,
):
    fetch = pltpu.make_async_copy(listed_hbm, listed_ref, sem)
    fetch.start()
    rank = off_ref.shape[1]

    clear_pads(iter_ref, 4)
    gram_ref[...] = jnp.zeros_like(gram_ref)
    left = fresh_left(inverse_factor(jnp.sum(grams_ref[...], 0), rank, total_points))

    fetch.wait()
    off, on = sides(listed_ref)
    held = ((off + 1, off_ref), (on + 1, on_ref), (3 * off, off_in_ref), (3 * on, on_in_ref))

    @pl.loop(0, COLW, unroll=4)
    def _(r):
        for column, ref in held:
            iter_ref[column * SLOTS + PAD + r] = fresh_of(left, ref[r]).astype(BF16)

    acc_ref[...] = jnp.zeros_like(acc_ref)
    moved = own_shift(listed_ref)
    shifts = halo_shifts(listed_ref)

    @pl.loop(0, COLW, unroll=4)
    def _(r):
        home = SLOTS + PAD + r
        own_apply(own_ref.at[r], iter_ref, acc_ref, home, home + SLOTS, home + SLOTS + moved - 1)
        for n, column in enumerate((off, on)):
            at = column * 3 * SLOTS + PAD + r + jnp.where(column == 0, *shifts) - 1
            total = times(iter_ref[at], halo_ref[r, n * 3])
            for k in range(1, 3):
                total = total + times(iter_ref[at + k], halo_ref[r, n * 3 + k])
            acc_ref[home + column * SLOTS] += total

    @pl.loop(0, COLW, unroll=8)
    def _(r):
        for column in range(2):
            total = acc_ref[(column + 1) * SLOTS + PAD + r]
            out_ref[column * COLW + r] = total
            gram_add(gram_ref, total)

    gram_out_ref[...] = jnp.broadcast_to(gram_packed(gram_ref, rank)[None], gram_out_ref.shape)


def last_kernel(total_points, grams_ref, applied_ref, out_hbm, out_ref, sem):
    tiles, rank = applied_ref.shape[:2]
    left = fresh_left(inverse_factor(jnp.sum(grams_ref[...], 0), rank, total_points))
    share = tiles // sem.shape[0]
    sends = []
    for part in range(sem.shape[0]):
        rows = pl.ds(part * share, share)
        for tile in range(part * share, (part + 1) * share):
            out_ref[tile] = fresh_of(left, applied_ref[tile])
        sends.append(pltpu.make_async_copy(out_ref.at[rows], out_hbm.at[rows], sem.at[part]))
        sends[-1].start()
    for send in sends:
        send.wait()


def fold_kernel(in_ref, out_ref):
    out_ref[...] = jnp.broadcast_to(jnp.sum(in_ref[...], 0)[None], out_ref.shape)


def cost(flops, moved):
    return pl.CostEstimate(flops=flops, bytes_accessed=moved, transcendentals=0)


SMEM = pl.BlockSpec(memory_space=pltpu.SMEM)
VMEM = pl.BlockSpec(memory_space=pltpu.VMEM)
HBM = pl.BlockSpec(memory_space=pltpu.HBM)
PARAMS = pltpu.CompilerParams(vmem_limit_bytes=VMEM_LIMIT)
SMALL = pltpu.CompilerParams(vmem_limit_bytes=4 * 1024 * 1024)


def swapped(shard, first):
    lows = range(first, lax.axis_size(TILES_REP) - 1, 2)
    pairs = [pair for i in lows for pair in ((i, i + 1), (i + 1, i))]
    return lax.ppermute(shard, TILES_REP, pairs)


def exchanged(shard, axes):
    return lax.all_to_all(shard, axes, split_axis=0, concat_axis=0, tiled=True)


def gathered(copies, *beside):
    line = lax.axis_size(LINE)
    plane, *beside = lax.optimization_barrier((exchanged(copies, PLANE), *beside))
    summed = pl.pallas_call(
        fold_kernel,
        out_shape=jax.ShapeDtypeStruct((line, *copies.shape[1:]), F32),
        in_specs=[VMEM],
        out_specs=VMEM,
        compiler_params=SMALL,
        name="fold",
    )(plane)
    beside = [swapped(x, 1 - n) for n, x in enumerate(beside)]
    return exchanged(summed, LINE), *beside


def local(members, initial, wet_counts, tile_coords, neighbours):
    tiles, count, points = members.shape
    rank = initial.shape[1]
    assert tiles == 2 * COLW and points == SIDE * SIDE and rank == 32
    shape = jax.ShapeDtypeStruct
    total_points = float(tiles * lax.axis_size(TILES_REP) * points)
    plane = lax.axis_size(PLANE)
    packed = (8, rank * rank // 8)

    members, initial, wet_counts, neighbours = (
        pltpu.with_memory_space_constraint(x, pltpu.HBM) for x in (members, initial, wet_counts, neighbours)
    )
    pair_s = shape((COLW, count + rank, points), BF16)
    off, on = pl.pallas_call(
        pack_kernel,
        out_shape=(pair_s, pair_s),
        in_specs=[SMEM, SMEM, VMEM, VMEM],
        out_specs=(VMEM, VMEM),
        compiler_params=SMALL,
        name="pack",
    )(wet_counts, neighbours, members, initial)
    off_in, on_in = swapped(off, 1), swapped(on, 0)

    table_s, padded_s = shape((9, points, points), F32), shape((tiles, DEPTH, points), BF16)
    own_s, part_s = shape((COLW, 7, points, points), BF16), shape((2 * SLOTS, rank, points), F32)
    halo_s, half_s = shape((COLW, 6, points, points), BF16), shape((COLW, rank, points), F32)
    listed_s = (pltpu.SMEM(neighbours.shape, jnp.int32), pltpu.SemaphoreType.DMA)
    turned_s = pltpu.VMEM((2 * SLOTS, points, DEPTH), BF16)
    table, padded, own_blocks, part = pl.pallas_call(
        own_kernel,
        out_shape=(table_s, padded_s, own_s, part_s),
        in_specs=[HBM, VMEM, VMEM],
        out_specs=(VMEM,) * 4,
        scratch_shapes=[
            pltpu.VMEM((3, SIDE, 64 * SIDE), F32),
            turned_s,
            pltpu.VMEM((2 * SLOTS, rank, points), BF16),
            *listed_s,
        ],
        compiler_params=PARAMS,
        cost_estimate=cost(96 * 2 * points * points * (DEPTH + rank), 40_000_000),
        name="own_blocks",
    )(neighbours, off, on)

    halo_blocks, off, on, copies = pl.pallas_call(
        halo_kernel,
        out_shape=(halo_s, half_s, half_s, shape((plane, *packed), F32)),
        in_specs=[HBM] + [VMEM] * 5,
        out_specs=(VMEM,) * 4,
        scratch_shapes=[
            turned_s,
            pltpu.VMEM((2 * SLOTS, rank, points), BF16),
            pltpu.VMEM((2, rank, points), F32),
            pltpu.VMEM((3 * rank, 3 * rank), F32),
            *listed_s,
        ],
        compiler_params=PARAMS,
        cost_estimate=cost(48 * 2 * points * points * (DEPTH + rank), 20_000_000),
        name="halo_blocks",
    )(neighbours, padded, table, part, off_in, on_in)

    grams, off_in, on_in = gathered(copies, off, on)
    applied, copies = pl.pallas_call(
        functools.partial(again_kernel, total_points),
        out_shape=(shape((tiles, rank, points), F32), shape((plane, *packed), F32)),
        in_specs=[HBM] + [VMEM] * 7,
        out_specs=(VMEM, VMEM),
        scratch_shapes=[
            pltpu.VMEM((4 * SLOTS, rank, points), BF16),
            pltpu.VMEM((4 * SLOTS, rank, points), F32),
            pltpu.VMEM((3 * rank, 3 * rank), F32),
            *listed_s,
        ],
        compiler_params=pltpu.CompilerParams(vmem_limit_bytes=24 * 1024 * 1024),
        name="apply_again",
    )(neighbours, grams, off, on, off_in, on_in, own_blocks, halo_blocks)

    return pl.pallas_call(
        functools.partial(last_kernel, total_points),
        out_shape=shape((tiles, rank, points), F32),
        in_specs=[VMEM, VMEM],
        out_specs=HBM,
        scratch_shapes=[pltpu.VMEM((tiles, rank, points), F32), pltpu.SemaphoreType.DMA((4,))],
        compiler_params=SMALL,
        name="last_fresh",
    )(*gathered(copies), applied)


def solution(mesh):
    split = Mesh(mesh.devices.reshape(*SPLIT, mesh.shape["rep"]), TILES_REP)
    return jax.shard_map(
        local,
        mesh=split,
        in_specs=(
            P(TILES_REP, None, None),
            P(TILES_REP, None, None),
            P(TILES_REP),
            P(TILES_REP, None),
            P(TILES_REP, None),
        ),
        out_specs=P(TILES_REP, None, None),
        check_vma=False,
    )
```

```python
import functools

import jax
import jax.numpy as jnp
from jax import lax
from jax.experimental import pallas as pl
from jax.experimental.pallas import tpu as pltpu
from jax.sharding import Mesh
from jax.sharding import PartitionSpec as P

SIDE = 16
COLW = 8
SPLIT = (4, 16, 4)
TILES_REP = ("tiles_0", "tiles_1", "tiles_2", "rep")
PLANE = ("tiles_0", "tiles_2", "rep")
LINE = ("tiles_1",)
PAD = 2
SLOTS = COLW + 2 * PAD
DEPTH = 128
F32 = jnp.float32
BF16 = jnp.bfloat16
VMEM_LIMIT = 20 * 1024 * 1024


def gaspari(scaled):
    clamped = jnp.maximum(scaled, 1.0)
    inner = (((-0.25 * scaled + 0.5) * scaled + 0.625) * scaled - 5.0 / 3.0) * scaled * scaled + 1.0
    outer = (
        ((((scaled / 12.0 - 0.5) * scaled + 0.625) * scaled + 5.0 / 3.0) * scaled - 5.0) * scaled
        + 4.0
        - 2.0 / (3.0 * clamped)
    )
    return jnp.where(scaled <= 1.0, inner, jnp.where(scaled <= 2.0, outer, 0.0))


def make_tapers(table_ref, wide_ref, members):
    shape = (SIDE, 64 * SIDE)
    lane = lax.broadcasted_iota(jnp.int32, shape, 1)
    sub = lax.broadcasted_iota(jnp.int32, shape, 0)
    apart_row = (2 * SIDE - 1 - lane // SIDE).astype(F32)
    for k in range(3):
        apart_col = (SIDE * (k - 1) + sub - lane % SIDE).astype(F32)
        distance = jnp.sqrt(apart_row * apart_row + apart_col * apart_col)
        wide_ref[k] = gaspari(distance / (0.5 * SIDE)) / (members - 1.0)
    per_group = 128 // SIDE
    for k in range(3):
        wide = wide_ref[k]
        for turn in range(per_group):
            rolled = pltpu.roll(wide, 64 * SIDE - turn * SIDE, 1) if turn else wide
            for d in range(3):
                for row in range(SIDE):
                    first = 2 * SIDE - 1 - SIDE * (d - 1) - row
                    if first % per_group == turn and (d, k) != (1, 0):
                        start = (first - turn) * SIDE
                        table_ref[d * 3 + k, row * SIDE : (row + 1) * SIDE, :] = rolled[
                            :, start : start + SIDE * SIDE
                        ]


def split3(x):
    high = x.astype(BF16)
    rest = x - high.astype(F32)
    mid = rest.astype(BF16)
    low = (rest - mid.astype(F32)).astype(BF16)
    return high, mid, low


def make_blocks(turned_ref, at, right, tables, block_ref, first):
    points = right.shape[1]
    count = len(tables)
    for n, table in enumerate(tables):
        product = jnp.dot(turned_ref[at + n], right, preferred_element_type=F32)
        block_ref[first + n] = (product * table[...]).astype(BF16)


def times(rows, block):
    return jnp.dot(rows, block, preferred_element_type=F32)


def times_turned(rows, block):
    return lax.dot_general(rows, block, (((1,), (1,)), ((), ())), preferred_element_type=F32)


def gram_add(gram_ref, applied):
    parts = jnp.concatenate(split3(applied), 0)
    gram_ref[...] += lax.dot_general(parts, parts, (((1,), (1,)), ((), ())), preferred_element_type=F32)


def gram_packed(gram_ref, rank):
    full = gram_ref[...]

    def piece(a, b):
        return full[a * rank : (a + 1) * rank, b * rank : (b + 1) * rank]

    small = piece(0, 2) + piece(2, 0) + piece(1, 1) + (piece(1, 2) + piece(2, 1))
    total = piece(0, 0) + (piece(0, 1) + piece(1, 0) + small)
    return jnp.concatenate([total[8 * q : 8 * q + 8, :] for q in range(rank // 8)], 1)


def inverse_factor(packed, rank, total_points):
    gram = jnp.concatenate([packed[:, rank * q : rank * (q + 1)] for q in range(rank // 8)], 0)
    gram = gram / total_points
    work = jnp.concatenate([gram, jnp.zeros((rank, 128 - rank), F32)], 1)
    lane = lax.broadcasted_iota(jnp.int32, (rank, 128), 1)
    sub = lax.broadcasted_iota(jnp.int32, (rank, 128), 0)
    work = jnp.where(lane == sub + rank, 1.0, work)
    groups = []
    for step in range(0, rank, 4):
        base = step // 8 * 8
        at = step - base
        below = work[base:, :]
        columns = [jnp.broadcast_to(below[:, step + j : step + j + 1], below.shape) for j in range(4)]

        def pivot(i, j):
            return columns[j][at + i : at + i + 1, :]

        r0, r1, r2, r3 = (below[at + i : at + i + 1, :] for i in range(4))
        a00, a10, a11 = pivot(0, 0), pivot(1, 0), pivot(1, 1)
        over = 1.0 / (a00 * a11 - a10 * a10)
        i00, i10, i11 = a11 * over, -a10 * over, a00 * over
        b00, b01, b10, b11 = pivot(2, 0), pivot(2, 1), pivot(3, 0), pivot(3, 1)
        y00, y01 = b00 * i00 + b01 * i10, b00 * i10 + b01 * i11
        y10, y11 = b10 * i00 + b11 * i10, b10 * i10 + b11 * i11
        s00 = pivot(2, 2) - (y00 * b00 + y01 * b01)
        s10 = pivot(3, 2) - (y10 * b00 + y11 * b01)
        s11 = pivot(3, 3) - (y10 * b10 + y11 * b11)
        w2 = r2 - (y00 * r0 + y01 * r1)
        w3 = r3 - (y10 * r0 + y11 * r1)
        q1, q3 = a10 / a00, s10 / s00
        done = (
            r0 / jnp.sqrt(a00),
            (r1 - q1 * r0) / jnp.sqrt(a11 - q1 * a10),
            w2 / jnp.sqrt(s00),
            (w3 - q3 * w2) / jnp.sqrt(s11 - q3 * s10),
        )
        if at == 0:
            groups.append(jnp.zeros((8, 128), F32))
        for i in range(4):
            groups[-1] = jnp.where(sub[:8, :] == at + i, done[i], groups[-1])
        if step + 4 < rank:
            over = 1.0 / (s00 * s11 - s10 * s10)
            z2 = (s11 * w2 - s10 * w3) * over
            z3 = (s00 * w3 - s10 * w2) * over
            z0 = i00 * r0 + i10 * r1 - (y00 * z2 + y10 * z3)
            z1 = i10 * r0 + i11 * r1 - (y01 * z2 + y11 * z3)
            left = below - (columns[0] * z0 + columns[1] * z1) - (columns[2] * z2 + columns[3] * z3)
            if at == 0:
                left = jnp.where(sub[base:, :] > step + 3, left, below)
            work = jnp.concatenate([work[:base, :], left], 0) if base else left
    return jnp.concatenate(groups, 0)[:, rank : 2 * rank]


def fresh_left(inverse):
    h1, h2, h3 = split3(inverse)
    return jnp.concatenate([h1, h1, h2, h1, h2, h3, h2, h3], 1)


def fresh_of(left, applied):
    a1, a2, a3 = split3(applied)
    right = jnp.concatenate([a1, a2, a1, a3, a2, a1, a3, a2], 0)
    return jnp.dot(left, right, preferred_element_type=F32)


def clear_pads(ref, columns):
    for column in range(columns):
        for slot in list(range(PAD)) + list(range(SLOTS - PAD, SLOTS)):
            ref[column * SLOTS + slot] = jnp.zeros(ref.shape[1:], ref.dtype)


def turn_in(turned_ref, at, rows):
    depth = rows.shape[0]
    padded = jnp.concatenate([rows, jnp.zeros((DEPTH - depth, rows.shape[1]), F32)], 0)
    turned_ref[at] = jnp.transpose(padded).astype(BF16)
    return padded.astype(BF16)


def own_shift(listed_ref):
    middle = COLW + COLW // 2 - 1
    return -jnp.clip(listed_ref[middle, 0] - listed_ref[middle, 3] + COLW, -1, 1)


def halo_shifts(listed_ref):
    middle = COLW // 2 - 1
    before = listed_ref[middle, 0] - listed_ref[middle, 3] + COLW
    after = listed_ref[COLW + middle, 8] - listed_ref[COLW + middle, 5] - COLW
    return jnp.clip(before, -1, 1), jnp.clip(after, -1, 1)


def own_apply(blocks, iter_ref, acc_ref, home, other, across):
    left, right = iter_ref[home], iter_ref[other]
    total = times(left, blocks[0]) + times(iter_ref[home + 1], blocks[1])
    for k in range(3):
        total = total + times(iter_ref[across + k], blocks[2 + k])
    acc_ref[home] += total
    acc_ref[home + 1] += times_turned(left, blocks[1])
    for k in range(3):
        acc_ref[across + k] += times_turned(left, blocks[2 + k])
    acc_ref[other] += times(right, blocks[5]) + times(iter_ref[other + 1], blocks[6])
    acc_ref[other + 1] += times_turned(right, blocks[6])


def sides(listed_ref):
    own_id = listed_ref[COLW + COLW // 2 - 1, 4]
    core = lax.rem(lax.div(own_id, 2 * COLW), 2)
    return core, 1 - core


def pack_kernel(wet_ref, listed_ref, members_ref, initial_ref, off_ref, on_ref):
    count = members_ref.shape[1]
    lane = lax.broadcasted_iota(jnp.int32, members_ref.shape[1:], 1)

    @pl.loop(0, COLW, unroll=8)
    def _(tile):
        for column, ref in zip(sides(listed_ref), (off_ref, on_ref)):
            at = column * COLW + tile
            rows = jnp.where(lane < wet_ref[at], members_ref[at].astype(F32), 0.0)
            ref[tile, :count, :] = rows.astype(BF16)
            ref[tile, count:, :] = initial_ref[at]


def own_kernel(
    listed_hbm, off_ref, on_ref,
    table_ref, padded_ref, block_ref, part_ref,
    wide_ref, turned_ref, iter_ref, listed_ref, sem,
):
    fetch = pltpu.make_async_copy(listed_hbm, listed_ref, sem)
    fetch.start()
    count = off_ref.shape[1] - iter_ref.shape[1]
    make_tapers(table_ref, wide_ref, float(count))
    clear_pads(turned_ref, 2)
    clear_pads(iter_ref, 2)
    part_ref[...] = jnp.zeros_like(part_ref)

    fetch.wait()

    @pl.loop(0, COLW, unroll=8)
    def _(tile):
        for column, ref in zip(sides(listed_ref), (off_ref, on_ref)):
            at = column * SLOTS + PAD + tile
            padded_ref[column * COLW + tile] = turn_in(turned_ref, at, ref[tile, :count, :].astype(F32))
            iter_ref[at] = ref[tile, count:, :]

    moved = own_shift(listed_ref)
    same, next_up = table_ref.at[4], table_ref.at[5]

    @pl.loop(0, COLW, unroll=8)
    def _(r):
        home = PAD + r
        other = SLOTS + PAD + r
        across = other + moved - 1
        blocks = block_ref.at[r]
        left = padded_ref[r]
        make_blocks(turned_ref, home, left, (same, next_up), blocks, 0)
        make_blocks(turned_ref, across, left, [table_ref.at[6 + k] for k in range(3)], blocks, 2)
        make_blocks(turned_ref, other, padded_ref[COLW + r], (same, next_up), blocks, 5)
        own_apply(blocks, iter_ref, part_ref, home, other, across)


def halo_kernel(
    listed_hbm, padded_ref, table_ref, part_ref, off_in_ref, on_in_ref,
    block_ref, off_out_ref, on_out_ref, gram_out_ref,
    turned_ref, iter_ref, last_ref, gram_ref, listed_ref, sem,
):
    fetch = pltpu.make_async_copy(listed_hbm, listed_ref, sem)
    fetch.start()
    rank = iter_ref.shape[1]
    count = off_in_ref.shape[1] - rank
    clear_pads(turned_ref, 2)
    clear_pads(iter_ref, 2)
    gram_ref[...] = jnp.zeros_like(gram_ref)
    last_ref[...] = jnp.zeros_like(last_ref)

    @pl.loop(0, COLW, unroll=8)
    def _(tile):
        for n, ref in enumerate((off_in_ref, on_in_ref)):
            at = n * SLOTS + PAD + tile
            turn_in(turned_ref, at, ref[tile, :count, :].astype(F32))
            iter_ref[at] = ref[tile, count:, :]

    fetch.wait()
    shifts = halo_shifts(listed_ref)
    columns = sides(listed_ref)

    @pl.loop(0, COLW, unroll=8)
    def _(r):
        for n, column in enumerate(columns):
            at = n * SLOTS + PAD + r + jnp.where(column == 0, *shifts) - 1
            make_blocks(
                turned_ref, at, padded_ref[column * COLW + r],
                [table_ref.at[6 * column + k] for k in range(3)], block_ref.at[r], n * 3,
            )
        for n, (column, out_ref) in enumerate(zip(columns, (off_out_ref, on_out_ref))):
            at = n * SLOTS + PAD + r + jnp.where(column == 0, *shifts) - 1
            total = part_ref[column * SLOTS + PAD + r]
            for k in range(3):
                total = total + times(iter_ref[at + k], block_ref[r, n * 3 + k])
            out_ref[r] = total
            gram_add(gram_ref, last_ref[n])
            last_ref[n] = total

    for column in range(2):
        gram_add(gram_ref, last_ref[column])
    gram_out_ref[...] = jnp.broadcast_to(gram_packed(gram_ref, rank)[None], gram_out_ref.shape)


def again_kernel(
    total_points,
    listed_hbm, grams_ref, off_ref, on_ref, off_in_ref, on_in_ref, own_ref, halo_ref,
    out_ref, gram_out_ref,
    iter_ref, acc_ref, gram_ref, listed_ref, sem,
):
    fetch = pltpu.make_async_copy(listed_hbm, listed_ref, sem)
    fetch.start()
    rank = off_ref.shape[1]

    clear_pads(iter_ref, 4)
    gram_ref[...] = jnp.zeros_like(gram_ref)
    left = fresh_left(inverse_factor(jnp.sum(grams_ref[...], 0), rank, total_points))

    fetch.wait()
    off, on = sides(listed_ref)
    held = ((off + 1, off_ref), (on + 1, on_ref), (3 * off, off_in_ref), (3 * on, on_in_ref))

    @pl.loop(0, COLW, unroll=4)
    def _(r):
        for column, ref in held:
            iter_ref[column * SLOTS + PAD + r] = fresh_of(left, ref[r]).astype(BF16)

    acc_ref[...] = jnp.zeros_like(acc_ref)
    moved = own_shift(listed_ref)
    shifts = halo_shifts(listed_ref)

    @pl.loop(0, COLW, unroll=4)
    def _(r):
        home = SLOTS + PAD + r
        own_apply(own_ref.at[r], iter_ref, acc_ref, home, home + SLOTS, home + SLOTS + moved - 1)
        for n, column in enumerate((off, on)):
            at = column * 3 * SLOTS + PAD + r + jnp.where(column == 0, *shifts) - 1
            total = times(iter_ref[at], halo_ref[r, n * 3])
            for k in range(1, 3):
                total = total + times(iter_ref[at + k], halo_ref[r, n * 3 + k])
            acc_ref[home + column * SLOTS] += total

    @pl.loop(0, COLW, unroll=8)
    def _(r):
        for column in range(2):
            total = acc_ref[(column + 1) * SLOTS + PAD + r]
            out_ref[column * COLW + r] = total
            gram_add(gram_ref, total)

    gram_out_ref[...] = jnp.broadcast_to(gram_packed(gram_ref, rank)[None], gram_out_ref.shape)


def last_kernel(total_points, grams_ref, applied_ref, out_hbm, out_ref, sem):
    tiles, rank = applied_ref.shape[:2]
    left = fresh_left(inverse_factor(jnp.sum(grams_ref[...], 0), rank, total_points))
    share = tiles // sem.shape[0]
    sends = []
    for part in range(sem.shape[0]):
        rows = pl.ds(part * share, share)
        for tile in range(part * share, (part + 1) * share):
            out_ref[tile] = fresh_of(left, applied_ref[tile])
        sends.append(pltpu.make_async_copy(out_ref.at[rows], out_hbm.at[rows], sem.at[part]))
        sends[-1].start()
    for send in sends:
        send.wait()


def fold_kernel(in_ref, out_ref):
    out_ref[...] = jnp.broadcast_to(jnp.sum(in_ref[...], 0)[None], out_ref.shape)


def cost(flops, moved):
    return pl.CostEstimate(flops=flops, bytes_accessed=moved, transcendentals=0)


SMEM = pl.BlockSpec(memory_space=pltpu.SMEM)
VMEM = pl.BlockSpec(memory_space=pltpu.VMEM)
HBM = pl.BlockSpec(memory_space=pltpu.HBM)
PARAMS = pltpu.CompilerParams(vmem_limit_bytes=VMEM_LIMIT)
SMALL = pltpu.CompilerParams(vmem_limit_bytes=4 * 1024 * 1024)


def swapped(shard, first):
    lows = range(first, lax.axis_size(TILES_REP) - 1, 2)
    pairs = [pair for i in lows for pair in ((i, i + 1), (i + 1, i))]
    return lax.ppermute(shard, TILES_REP, pairs)


def exchanged(shard, axes):
    return lax.all_to_all(shard, axes, split_axis=0, concat_axis=0, tiled=True)


def gathered(copies, *beside):
    line = lax.axis_size(LINE)
    plane, *beside = lax.optimization_barrier((exchanged(copies, PLANE), *beside))
    summed = pl.pallas_call(
        fold_kernel,
        out_shape=jax.ShapeDtypeStruct((line, *copies.shape[1:]), F32),
        in_specs=[VMEM],
        out_specs=VMEM,
        compiler_params=SMALL,
        name="fold",
    )(plane)
    return exchanged(summed, LINE), *beside


def local(members, initial, wet_counts, tile_coords, neighbours):
    tiles, count, points = members.shape
    rank = initial.shape[1]
    assert tiles == 2 * COLW and points == SIDE * SIDE and rank == 32
    shape = jax.ShapeDtypeStruct
    total_points = float(tiles * lax.axis_size(TILES_REP) * points)
    plane = lax.axis_size(PLANE)
    packed = (8, rank * rank // 8)

    members, initial, wet_counts, neighbours = (
        pltpu.with_memory_space_constraint(x, pltpu.HBM) for x in (members, initial, wet_counts, neighbours)
    )
    pair_s = shape((COLW, count + rank, points), BF16)
    off, on = pl.pallas_call(
        pack_kernel,
        out_shape=(pair_s, pair_s),
        in_specs=[SMEM, SMEM, VMEM, VMEM],
        out_specs=(VMEM, VMEM),
        compiler_params=SMALL,
        name="pack",
    )(wet_counts, neighbours, members, initial)
    off_in, on_in = swapped(off, 1), swapped(on, 0)

    table_s, padded_s = shape((9, points, points), F32), shape((tiles, DEPTH, points), BF16)
    own_s, part_s = shape((COLW, 7, points, points), BF16), shape((2 * SLOTS, rank, points), F32)
    halo_s, half_s = shape((COLW, 6, points, points), BF16), shape((COLW, rank, points), F32)
    listed_s = (pltpu.SMEM(neighbours.shape, jnp.int32), pltpu.SemaphoreType.DMA)
    turned_s = pltpu.VMEM((2 * SLOTS, points, DEPTH), BF16)
    table, padded, own_blocks, part = pl.pallas_call(
        own_kernel,
        out_shape=(table_s, padded_s, own_s, part_s),
        in_specs=[HBM, VMEM, VMEM],
        out_specs=(VMEM,) * 4,
        scratch_shapes=[
            pltpu.VMEM((3, SIDE, 64 * SIDE), F32),
            turned_s,
            pltpu.VMEM((2 * SLOTS, rank, points), BF16),
            *listed_s,
        ],
        compiler_params=PARAMS,
        cost_estimate=cost(96 * 2 * points * points * (DEPTH + rank), 40_000_000),
        name="own_blocks",
    )(neighbours, off, on)

    halo_blocks, off, on, copies = pl.pallas_call(
        halo_kernel,
        out_shape=(halo_s, half_s, half_s, shape((plane, *packed), F32)),
        in_specs=[HBM] + [VMEM] * 5,
        out_specs=(VMEM,) * 4,
        scratch_shapes=[
            turned_s,
            pltpu.VMEM((2 * SLOTS, rank, points), BF16),
            pltpu.VMEM((2, rank, points), F32),
            pltpu.VMEM((3 * rank, 3 * rank), F32),
            *listed_s,
        ],
        compiler_params=PARAMS,
        cost_estimate=cost(48 * 2 * points * points * (DEPTH + rank), 20_000_000),
        name="halo_blocks",
    )(neighbours, padded, table, part, off_in, on_in)

    grams, off_in, on_in = gathered(copies, swapped(off, 1), swapped(on, 0))
    applied, copies = pl.pallas_call(
        functools.partial(again_kernel, total_points),
        out_shape=(shape((tiles, rank, points), F32), shape((plane, *packed), F32)),
        in_specs=[HBM] + [VMEM] * 7,
        out_specs=(VMEM, VMEM),
        scratch_shapes=[
            pltpu.VMEM((4 * SLOTS, rank, points), BF16),
            pltpu.VMEM((4 * SLOTS, rank, points), F32),
            pltpu.VMEM((3 * rank, 3 * rank), F32),
            *listed_s,
        ],
        compiler_params=pltpu.CompilerParams(vmem_limit_bytes=24 * 1024 * 1024),
        name="apply_again",
    )(neighbours, grams, off, on, off_in, on_in, own_blocks, halo_blocks)

    return pl.pallas_call(
        functools.partial(last_kernel, total_points),
        out_shape=shape((tiles, rank, points), F32),
        in_specs=[VMEM, VMEM],
        out_specs=HBM,
        scratch_shapes=[pltpu.VMEM((tiles, rank, points), F32), pltpu.SemaphoreType.DMA((4,))],
        compiler_params=SMALL,
        name="last_fresh",
    )(*gathered(copies), applied)


def solution(mesh):
    split = Mesh(mesh.devices.reshape(*SPLIT, mesh.shape["rep"]), TILES_REP)
    return jax.shard_map(
        local,
        mesh=split,
        in_specs=(
            P(TILES_REP, None, None),
            P(TILES_REP, None, None),
            P(TILES_REP),
            P(TILES_REP, None),
            P(TILES_REP, None),
        ),
        out_specs=P(TILES_REP, None, None),
        check_vma=False,
    )
```
